256 devices in a mesh: seq: 128 (over x_lo, y, z, core), head: 2 (over x_hi).
Axes of the slice: x: 4 (x_hi: 2, x_lo: 2; x = x_hi * 2 + x_lo), y: 4, z: 8, core: 2. Of those that a mesh axis runs over, the one named last changes fastest.
Arguments:
- query: bfloat16 [32768, 3584], P('seq', 'head'), may hold values from -6 to 6
- key: bfloat16 [32768, 512], P('seq', 'head'), may hold values from -6 to 6
- value: bfloat16 [32768, 512], P('seq', 'head'), may hold values from -6 to 6
- output: bfloat16 [32768, 3584], P('seq', 'head'), may hold values from -6 to 6
- output_gradient: bfloat16 [32768, 3584], P('seq', 'head'), may hold values from -6 to 6
- lse: float32 [28, 32768], P('head', 'seq'), may hold values from 3 to 6
- doc_lengths: int32 [32], replicated, may hold values from 1 to 2048, as said below
- w_query: bfloat16 [3584, 3584], P('seq', 'head'), may hold values from -0.09375 to 0.09375
- key_weight: bfloat16 [3584, 512], P('seq', 'head'), may hold values from -0.09375 to 0.09375
- value_weight: bfloat16 [3584, 512], P('seq', 'head'), may hold values from -0.09375 to 0.09375
Outputs:
- grad_input: bfloat16 [32768, 3584], P('seq', 'head')
The draws below stay inside these ranges and needn't reach their ends.
Inputs may be any that keep to these rules, and one draw needn't show every extreme that they name: `doc_lengths`: the documents lie end to end and fill the 32768 tokens of the pack; the first has 1024 tokens, and one of exactly 2048 tokens begins at token 15360.
All inputs are finite; a program needn't handle non-finite values.
Results may differ from the reference program's by a relative error of at most 0.0056.
Values may be sent and summed in bfloat16 or wider, within the bound.
A program may use at most 128 MiB of HBM per device.

```python
import math
import jax
import jax.numpy as jnp
from jax import lax

MODEL_WIDTH = 3584
HQ = 28
KEY_VALUE_HEADS = 4
HEAD_SIZE = 128
TOKENS_PER_SHARD = 256
QUERY_PER_KV = 7
WINDOW = 512
PACK_TOKENS = 32768
DOCS = 32
MAXDOC = 2048
N_SEQ = 128


def split_span(subkey, span, count):
    if count == 0:
        return jnp.zeros((0,), jnp.int32)
    if count == 1:
        return jnp.full((1,), span, jnp.int32)
    base = span // count
    shifts = jax.random.randint(subkey, (count - 1,), 0, base // 2 + 1, dtype=jnp.int32)
    zero_one = jnp.zeros((1,), jnp.int32)
    pieces = base + jnp.concatenate([shifts, zero_one]) - jnp.concatenate([zero_one, shifts])
    extra = jnp.concatenate([jnp.zeros((count - 1,), jnp.int32), jnp.full((1,), span - count * base, jnp.int32)])
    return pieces + extra


def draw_doc_lengths(key, part):
    blocks = PACK_TOKENS // TOKENS_PER_SHARD
    half_blocks = blocks // 2
    first_span = (half_blocks - 8) * TOKENS_PER_SHARD
    second_span = (half_blocks - 4) * TOKENS_PER_SHARD
    first_count = (half_blocks - 8) // 4
    second_count = DOCS - 2 - first_count
    first_part = split_span(jax.random.fold_in(key, 11), first_span, first_count)
    second_part = split_span(jax.random.fold_in(key, 23), second_span, second_count)
    head_doc = jnp.full((1,), 4 * TOKENS_PER_SHARD, jnp.int32)
    long_doc = jnp.full((1,), MAXDOC, jnp.int32)
    return jnp.concatenate([head_doc, first_part, long_doc, second_part]).astype(jnp.int32)


def block_levels(rng, shape, split, least, largest):
    loudness = 1.0
    for dim, parts in split:
        draws = jax.random.uniform(jax.random.fold_in(jax.random.fold_in(rng, 6), dim), (parts,), jnp.float32, least / len(split), largest / len(split))
        loudness = loudness * jnp.repeat(jnp.exp(draws), shape[dim] // parts).reshape((-1,) + (1,) * (len(shape) - 1 - dim))
    return loudness


def normal_values(stream_key, extent, deviation, bound, cuts=(), kind=jnp.bfloat16):
    entries = deviation * jax.random.normal(stream_key, extent, jnp.float32)
    if cuts:
        entries = entries * block_levels(stream_key, extent, cuts, -0.22, 0.18)
    return jnp.clip(entries, -bound, bound).astype(kind)


def setup_inputs(seed: int = 0) -> dict:
    key_list = jax.random.split(jax.random.key(seed), 11)
    query = normal_values(key_list[0], (PACK_TOKENS, HQ * HEAD_SIZE), 1.0, 6.0, ((0, 128), (1, 2)))
    key = normal_values(key_list[1], (PACK_TOKENS, KEY_VALUE_HEADS * HEAD_SIZE), 1.0, 6.0, ((0, 128), (1, 2)))
    value = normal_values(key_list[2], (PACK_TOKENS, KEY_VALUE_HEADS * HEAD_SIZE), 1.0, 6.0, ((0, 128), (1, 2)))
    output = normal_values(key_list[3], (PACK_TOKENS, HQ * HEAD_SIZE), 1.0, 6.0, ((0, 128), (1, 2)))
    output_gradient = normal_values(key_list[4], (PACK_TOKENS, HQ * HEAD_SIZE), 1.0, 6.0, ((0, 128), (1, 2)))
    lse = jnp.clip(3.0 + 3.0 * jax.random.uniform(key_list[5], (HQ, PACK_TOKENS), jnp.float32) ** block_levels(key_list[5], (HQ, PACK_TOKENS), ((0, 2), (1, 128)), -0.2, 0.2), 3.0, 6.0)
    doc_lengths = draw_doc_lengths(jax.random.fold_in(key_list[10], 71), 0)
    w_query = normal_values(key_list[7], (MODEL_WIDTH, HQ * HEAD_SIZE), MODEL_WIDTH ** -0.5, 0.09375, ((0, 128), (1, 2)))
    key_weight = normal_values(key_list[8], (MODEL_WIDTH, KEY_VALUE_HEADS * HEAD_SIZE), MODEL_WIDTH ** -0.5, 0.09375, ((0, 128), (1, 2)))
    value_weight = normal_values(key_list[9], (MODEL_WIDTH, KEY_VALUE_HEADS * HEAD_SIZE), MODEL_WIDTH ** -0.5, 0.09375, ((0, 128), (1, 2)))
    return dict(query=query, key=key, value=value, output=output, output_gradient=output_gradient, lse=lse, doc_lengths=doc_lengths, w_query=w_query, key_weight=key_weight, value_weight=value_weight)


def lower_bounds(positions, doc_lengths, window):
    starts = jnp.cumsum(doc_lengths, dtype=jnp.int32) - doc_lengths
    inside = starts[None, :] <= positions[:, None]
    doc_begin = lax.optimization_barrier(jnp.max(jnp.where(inside, starts[None, :], 0), axis=1))
    return jnp.maximum(doc_begin, positions - window + 1)

def attend(query_rows, key_row_block, value_row_block, visible, logsumexp_rows, output_grad_rows, row_delta, score_scale):
    q_full = query_rows.astype(jnp.float32)
    k_full = key_row_block.astype(jnp.float32)
    v_full = value_row_block.astype(jnp.float32)
    g_full = output_grad_rows.astype(jnp.float32)
    scores = jnp.einsum('tgjd,kgd->gjtk', q_full, k_full) * score_scale
    prob_full = jnp.where(visible[None, None], jnp.exp(scores - logsumexp_rows[..., None]), 0.0)
    prob_low = prob_full.astype(jnp.bfloat16)
    grad_val = jnp.einsum('gjtk,tgjd->kgd', prob_low.astype(jnp.float32), g_full)
    grad_prob = jnp.einsum('tgjd,kgd->gjtk', g_full, v_full)
    dscore = (prob_full * (grad_prob - row_delta[..., None]) * score_scale).astype(jnp.bfloat16)
    dscore_full = dscore.astype(jnp.float32)
    grad_qry = jnp.einsum('gjtk,kgd->tgjd', dscore_full, k_full)
    grad_key = jnp.einsum('gjtk,tgjd->kgd', dscore_full, q_full)
    return (grad_qry, grad_key, grad_val)

def reference(query, key, value, output, output_gradient, lse, doc_lengths, w_query, key_weight, value_weight):
    key_value_width = KEY_VALUE_HEADS * HEAD_SIZE
    score_scale = 1.0 / math.sqrt(HEAD_SIZE)
    pad_rows = 2 * TOKENS_PER_SHARD
    padded_keys = jnp.concatenate([jnp.zeros((pad_rows, key_value_width), key.dtype), key], 0)
    padded_values = jnp.concatenate([jnp.zeros((pad_rows, key_value_width), value.dtype), value], 0)

    def step(carry, block_idx):
        key_acc, value_acc = carry
        first_index = block_idx * TOKENS_PER_SHARD
        positions = first_index + jnp.arange(TOKENS_PER_SHARD, dtype=jnp.int32)
        lower = lower_bounds(positions, doc_lengths, WINDOW)
        key_pos = first_index - pad_rows + jnp.arange(3 * TOKENS_PER_SHARD, dtype=jnp.int32)
        visible = (key_pos[None, :] >= lower[:, None]) & (key_pos[None, :] <= positions[:, None])
        query_rows = lax.dynamic_slice_in_dim(query, first_index, TOKENS_PER_SHARD, 0).reshape(TOKENS_PER_SHARD, KEY_VALUE_HEADS, QUERY_PER_KV, HEAD_SIZE)
        output_rows = lax.dynamic_slice_in_dim(output, first_index, TOKENS_PER_SHARD, 0).reshape(TOKENS_PER_SHARD, KEY_VALUE_HEADS, QUERY_PER_KV, HEAD_SIZE)
        output_grad_rows = lax.dynamic_slice_in_dim(output_gradient, first_index, TOKENS_PER_SHARD, 0).reshape(TOKENS_PER_SHARD, KEY_VALUE_HEADS, QUERY_PER_KV, HEAD_SIZE)
        key_row_block = lax.dynamic_slice_in_dim(padded_keys, first_index, 3 * TOKENS_PER_SHARD, 0).reshape(3 * TOKENS_PER_SHARD, KEY_VALUE_HEADS, HEAD_SIZE)
        value_row_block = lax.dynamic_slice_in_dim(padded_values, first_index, 3 * TOKENS_PER_SHARD, 0).reshape(3 * TOKENS_PER_SHARD, KEY_VALUE_HEADS, HEAD_SIZE)
        logsumexp_rows = lax.dynamic_slice_in_dim(lse, first_index, TOKENS_PER_SHARD, 1).reshape(KEY_VALUE_HEADS, QUERY_PER_KV, TOKENS_PER_SHARD)
        row_delta = jnp.einsum('tgjd,tgjd->gjt', output_grad_rows.astype(jnp.float32), output_rows.astype(jnp.float32))
        grad_qry, grad_key, grad_val = attend(query_rows, key_row_block, value_row_block, visible, logsumexp_rows, output_grad_rows, row_delta, score_scale)
        old_key = lax.dynamic_slice_in_dim(key_acc, first_index, 3 * TOKENS_PER_SHARD, 0)
        old_value = lax.dynamic_slice_in_dim(value_acc, first_index, 3 * TOKENS_PER_SHARD, 0)
        key_acc = lax.dynamic_update_slice_in_dim(key_acc, old_key + grad_key.reshape(3 * TOKENS_PER_SHARD, key_value_width), first_index, 0)
        value_acc = lax.dynamic_update_slice_in_dim(value_acc, old_value + grad_val.reshape(3 * TOKENS_PER_SHARD, key_value_width), first_index, 0)
        return ((key_acc, value_acc), grad_qry.reshape(TOKENS_PER_SHARD, HQ * HEAD_SIZE).astype(jnp.bfloat16))
    zero_acc = jnp.zeros((PACK_TOKENS + pad_rows, key_value_width), jnp.float32)
    (key_acc, value_acc), q_blocks = lax.scan(step, (zero_acc, zero_acc), jnp.arange(N_SEQ, dtype=jnp.int32))
    grad_query = q_blocks.reshape(PACK_TOKENS, HQ * HEAD_SIZE)
    grad_key = key_acc[pad_rows:].astype(jnp.bfloat16)
    grad_value = value_acc[pad_rows:].astype(jnp.bfloat16)
    total = jnp.dot(grad_query, w_query.T, preferred_element_type=jnp.float32)
    total = total + jnp.dot(grad_key, key_weight.T, preferred_element_type=jnp.float32)
    total = total + jnp.dot(grad_value, value_weight.T, preferred_element_type=jnp.float32)
    return total.astype(jnp.bfloat16)
```

```python
import math

import jax
import jax.numpy as jnp
from jax import lax
from jax.sharding import PartitionSpec as P

HEAD_SIZE = 128
WINDOW = 512


def shifted(array, axis, by):
    peers = lax.axis_size(axis)
    pairs = [(i, i + by) for i in range(peers) if 0 <= i + by < peers]
    return lax.ppermute(array, axis, pairs)


def lower_bounds(positions, doc_lengths, window):
    starts = jnp.cumsum(doc_lengths, dtype=jnp.int32) - doc_lengths
    inside = starts[None, :] <= positions[:, None]
    doc_begin = jnp.max(jnp.where(inside, starts[None, :], 0), axis=1)
    return jnp.maximum(doc_begin, positions - window + 1)


def attend(
    query_rows,
    key_row_block,
    value_row_block,
    visible,
    logsumexp_rows,
    output_grad_rows,
    row_delta,
    score_scale,
):
    scores = (
        jnp.einsum("tgjd,kgd->gjtk", query_rows, key_row_block, preferred_element_type=jnp.float32)
        * score_scale
    )
    prob_full = jnp.where(visible[None, None], jnp.exp(scores - logsumexp_rows[..., None]), 0.0)
    prob_low = prob_full.astype(jnp.bfloat16)
    grad_val = jnp.einsum(
        "gjtk,tgjd->kgd", prob_low, output_grad_rows, preferred_element_type=jnp.float32
    )
    grad_prob = jnp.einsum(
        "tgjd,kgd->gjtk", output_grad_rows, value_row_block, preferred_element_type=jnp.float32
    )
    dscore = (prob_full * (grad_prob - row_delta[..., None]) * score_scale).astype(jnp.bfloat16)
    grad_qry = jnp.einsum(
        "gjtk,kgd->tgjd", dscore, key_row_block, preferred_element_type=jnp.float32
    )
    grad_key = jnp.einsum("gjtk,tgjd->kgd", dscore, query_rows, preferred_element_type=jnp.float32)
    return (grad_qry, grad_key, grad_val)


def projector(grad_rows, w_piece):
    return jnp.einsum("tc,rc->tr", grad_rows, w_piece, preferred_element_type=jnp.float32)


def shards(
    query, key, value, output, output_gradient, lse, doc_lengths, w_query, key_weight, value_weight
):
    tok_rows = query.shape[0]
    key_value_width = key.shape[1]
    kv_heads = key_value_width // HEAD_SIZE
    q_heads = query.shape[1] // HEAD_SIZE
    per_group = q_heads // kv_heads
    score_scale = 1.0 / math.sqrt(HEAD_SIZE)
    seq_index = lax.axis_index("seq")
    positions = seq_index * tok_rows + jnp.arange(tok_rows, dtype=jnp.int32)
    lower = lower_bounds(positions, doc_lengths, WINDOW)
    query_rows = query.reshape(tok_rows, kv_heads, per_group, HEAD_SIZE)
    output_rows = output.reshape(tok_rows, kv_heads, per_group, HEAD_SIZE)
    output_grad_rows = output_gradient.reshape(tok_rows, kv_heads, per_group, HEAD_SIZE)
    row_delta = jnp.einsum(
        "tgjd,tgjd->gjt", output_grad_rows, output_rows, preferred_element_type=jnp.float32
    )
    logsumexp_rows = lse.reshape(kv_heads, per_group, tok_rows)
    near_pair = shifted((key, value), "seq", 1)
    far_pair = shifted((key, value), "seq", 2)
    key_all = jnp.concatenate([far_pair[0], near_pair[0], key], 0).reshape(
        3 * tok_rows, kv_heads, HEAD_SIZE
    )
    value_all = jnp.concatenate([far_pair[1], near_pair[1], value], 0).reshape(
        3 * tok_rows, kv_heads, HEAD_SIZE
    )
    key_pos = positions[0] - 2 * tok_rows + jnp.arange(3 * tok_rows, dtype=jnp.int32)
    visible = (key_pos[None, :] >= lower[:, None]) & (key_pos[None, :] <= positions[:, None])
    grad_qry, grad_key, grad_val = attend(
        query_rows,
        key_all,
        value_all,
        visible,
        logsumexp_rows,
        output_grad_rows,
        row_delta,
        score_scale,
    )
    key_parts = grad_key.reshape(3, tok_rows, key_value_width)
    value_parts = grad_val.reshape(3, tok_rows, key_value_width)
    key_far, key_near, key_own = (key_parts[0], key_parts[1], key_parts[2])
    value_far, value_near, value_own = (value_parts[0], value_parts[1], value_parts[2])
    back_near = shifted((key_near, value_near), "seq", -1)
    back_far = shifted((key_far, value_far), "seq", -2)
    key_total = key_own + back_near[0] + back_far[0]
    value_total = value_own + back_near[1] + back_far[1]
    q_grad_low = grad_qry.reshape(tok_rows, q_heads * HEAD_SIZE).astype(jnp.bfloat16)
    k_grad_low = key_total.astype(jnp.bfloat16)
    v_grad_low = value_total.astype(jnp.bfloat16)
    weights = jnp.concatenate([w_query, key_weight, value_weight], 1)
    gathered = lax.all_gather(weights, "seq", axis=0, tiled=True)
    grads = jnp.concatenate([q_grad_low, k_grad_low, v_grad_low], 1)
    partial_sum = projector(grads, gathered)
    summed = lax.psum_scatter(partial_sum, "head", scatter_dimension=1, tiled=True)
    return summed.astype(jnp.bfloat16)


def solution(mesh):
    in_specs = (
        P("seq", "head"),
        P("seq", "head"),
        P("seq", "head"),
        P("seq", "head"),
        P("seq", "head"),
        P("head", "seq"),
        P(),
        P("seq", "head"),
        P("seq", "head"),
        P("seq", "head"),
    )
    out_specs = P("seq", "head")
    return jax.shard_map(shards, mesh=mesh, in_specs=in_specs, out_specs=out_specs, check_vma=False)
```

```python
import functools
import math

import jax
import jax.numpy as jnp
from jax import lax
from jax.experimental import pallas as pl
from jax.experimental.pallas import tpu as pltpu
from jax.sharding import PartitionSpec as P

HEAD = 128
WINDOW = 512
NEG = -1e30
LOG2E = math.log2(math.e)
F32 = jnp.float32
BF16 = jnp.bfloat16

NY, NZ = 4, 8
LINK = 46.5e3
HOP = 1.8
NT = (((1,), (1,)), ((), ()))


def chunk_sends(part, my, mz):
    out = []
    z_up = ("z", 1, my, (mz + 1) % NZ)
    z_dn = ("z", -1, my, (mz - 1) % NZ)
    y_up = ("y", 1, (my + 1) % NY, mz)
    y_dn = ("y", -1, (my - 1) % NY, mz)
    z_ups = mz <= 3
    z_dns = mz == 0 or mz in (6, 7)
    y_ups = my <= 1
    y_dns = my == 0
    if part == 1:
        if my == 0:
            out += [z_up] if z_ups else []
            out += [z_dn] if z_dns else []
        out += [y_up] if y_ups else []
        out += [y_dn] if y_dns else []
    else:
        if mz == 0:
            out += [y_up] if y_ups else []
            out += [y_dn] if y_dns else []
        out += [z_up] if z_ups else []
        out += [z_dn] if z_dns else []
    return out


def event_plan(size0, size1):
    size = (size0, size1)
    free = {("z", 1): 0.0, ("z", -1): 0.0, ("y", 1): 0.0, ("y", -1): 0.0}
    pending = [(0.0, 1, 0, 0), (0.0, 0, 0, 0)]
    order = []
    while pending:
        pending.sort()
        t, part, my, mz = pending.pop(0)
        order.append((t, part, my, mz))
        for axis, way, ry, rz in chunk_sends(part, my, mz):
            start = max(t, free[axis, way])
            done = start + size[part] / LINK
            free[axis, way] = done
            pending.append((done + HOP, part, ry, rz))
    return order


def kernel(
    plan,
    q_hbm, k_hbm, v_hbm, o_hbm, do_hbm, lse_hbm, dl_ref, wq_hbm, wk_hbm, wv_hbm,
    out_ref,
    qv, ov, dov, kb, vb, kt, bias, stat, lse_v, dq, gt, dk, dv, gsend, grecv,
    st, stf, wa, wb, res, psend, precv, oacc,
    in_sem, kv_send, kv_recv, st_send, st_recv, ici_recv, sib_recv,
    ici_send, sib_send, g_send, g_recv, p_send, p_recv,
):
    tok = qv.shape[0]
    heads = qv.shape[1] // HEAD
    groups = kb.shape[2] // HEAD
    per = heads // groups
    rows = st.shape[1]
    half = 2 * rows
    scale = 1.0 / math.sqrt(HEAD)
    wq_w, wk_w = wq_hbm.shape[1], wk_hbm.shape[1]

    me = lax.axis_index("seq")
    hd = lax.axis_index("head")
    n = NY * NZ * 4
    core = lax.rem(me, 2)
    zc = lax.rem(me // 2, NZ)
    yc = lax.rem(me // (2 * NZ), NY)
    xc = me // (2 * NZ * NY)
    sg = 1 - 2 * core
    slot_me = yc * NZ + zc
    piece_me = xc * 2 + core

    def at(x, y, z, c):
        return ((x * NY + y) * NZ + z) * 2 + c

    def zn(d):
        return at(xc, yc, lax.rem(zc + d * sg + NZ, NZ), core)

    def yn(d):
        return at(xc, lax.rem(yc + d * sg + NY, NY), zc, core)

    def slot_of(my, mz):
        y = lax.rem(yc - my * sg + NY, NY)
        z = lax.rem(zc - mz * sg + NZ, NZ)
        return y * NZ + z

    sib = at(xc, yc, zc, 1 - core)
    xsame = at(1 - xc, yc, zc, core)
    xother = at(1 - xc, yc, zc, 1 - core)
    nxt1, nxt2 = lax.rem(me + 1, n), lax.rem(me + 2, n)
    prv1, prv2 = lax.rem(me + n - 1, n), lax.rem(me + n - 2, n)

    barrier = pltpu.get_barrier_semaphore()
    partners = [sib, xsame, xother, zn(1), zn(-1), yn(1), yn(-1), nxt1, nxt2, prv1, prv2]
    for d in partners:
        pl.semaphore_signal(barrier, inc=1, device_id={"seq": d}, device_id_type=pl.DeviceIdType.MESH)
    pl.semaphore_signal(barrier, inc=1, device_id={"head": 1 - hd}, device_id_type=pl.DeviceIdType.MESH)

    locals_ = [
        pltpu.make_async_copy(k_hbm, kb.at[0], in_sem.at[0]),
        pltpu.make_async_copy(v_hbm, vb.at[0], in_sem.at[1]),
        pltpu.make_async_copy(do_hbm, dov, in_sem.at[2]),
        pltpu.make_async_copy(o_hbm, ov, in_sem.at[3]),
        pltpu.make_async_copy(q_hbm, qv, in_sem.at[4]),
        pltpu.make_async_copy(lse_hbm, lse_v, in_sem.at[5]),
    ]
    w_src = [(wq_hbm, 0, wq_w), (wk_hbm, wq_w, wk_w), (wv_hbm, wq_w + wk_w, wk_w)]
    w_own = [
        pltpu.make_async_copy(s, st.at[piece_me, :, pl.ds(o, w)], in_sem.at[6 + j])
        for j, (s, o, w) in enumerate(w_src)
    ]
    for c in w_own + locals_:
        c.start()

    pl.semaphore_wait(barrier, len(partners) + 1)

    def remote(src, dst, ssem, rsem, dev):
        return pltpu.make_async_remote_copy(
            src_ref=src, dst_ref=dst, send_sem=ssem, recv_sem=rsem,
            device_id=dev, device_id_type=pl.DeviceIdType.MESH,
        )

    stage = []
    for pi, dev in enumerate((xsame, xother, sib)):
        for j, (s, o, w) in enumerate(w_src):
            c = remote(s, st.at[piece_me, :, pl.ds(o, w)], st_send.at[3 * pi + j], st_recv.at[3 * pi + j], {"seq": dev})
            c.start()
            stage.append(c)
    halo = []
    for b, dev in ((1, nxt1), (2, nxt2)):
        for j, (s, d) in enumerate(((k_hbm, kb), (v_hbm, vb))):
            c = remote(s, d.at[b], kv_send.at[b - 1, j], kv_recv.at[b - 1, j], {"seq": dev})
            c.start()
            halo.append(c)

    qpos = me * tok + lax.broadcasted_iota(jnp.int32, (1, tok), 1)
    low = jnp.zeros((1, tok), jnp.int32)
    start = jnp.int32(0)
    for d in range(dl_ref.shape[0]):
        low = jnp.where(qpos >= start, start, low)
        start = start + dl_ref[d]
    low = jnp.maximum(low, qpos - (WINDOW - 1))
    for b in range(3):
        kpos = (me - b) * tok + lax.broadcasted_iota(jnp.int32, (tok, tok), 0)
        ok = (kpos >= low) & (kpos <= qpos)
        bias[b] = jnp.where(ok, 0.0, NEG).astype(F32)
    dk[...] = jnp.zeros_like(dk)
    dv[...] = jnp.zeros_like(dv)
    dq[...] = jnp.zeros_like(dq)

    for c in w_own:
        c.wait()
    for c in stage:
        c.wait_recv()
    for p in range(4):
        stf[pl.ds(p * rows, rows), :] = st[p].astype(F32)
    la, lb = wa.shape[3], wb.shape[3]
    for kh in range(2):
        base = kh * (la + lb)
        wb[kh, slot_me] = stf[:, pl.ds(base + la, lb)].astype(BF16)
        wa[kh, slot_me] = stf[:, pl.ds(base, la)].astype(BF16)

    def event(part, my, mz):
        buf = wb if part == 1 else wa
        slot = slot_of(my, mz)
        ref = buf.at[core, slot]
        if (my, mz) != (0, 0):
            remote(ref, ref, ici_send.at[part], ici_recv.at[part, my, mz], {"seq": sib}).wait_recv()
        for axis, way, ry, rz in chunk_sends(part, my, mz):
            dev = zn(way) if axis == "z" else yn(way)
            remote(ref, ref, ici_send.at[part], ici_recv.at[part, ry, rz], {"seq": dev}).start()
        if (my, mz) != (0, 0):
            remote(ref, ref, sib_send.at[part], sib_recv.at[part, my, mz], {"seq": sib}).start()

    attn_at, post = plan
    for ev in attn_at[-1]:
        event(*ev)

    for c in locals_:
        c.wait()

    def delta_step(h, _):
        cols = pl.ds(pl.multiple_of(h * HEAD, HEAD), HEAD)
        prod = dov[:, cols].astype(F32) * ov[:, cols].astype(F32)
        hi = prod.astype(BF16)
        lo = (prod - hi.astype(F32)).astype(BF16)
        one = jnp.ones((8, HEAD), BF16)
        tot = lax.dot_general(one, hi, NT, preferred_element_type=F32) + lax.dot_general(one, lo, NT, preferred_element_type=F32)
        stat[h] = tot
        return 0

    lax.fori_loop(0, heads, delta_step, 0)
    lse_v[...] = lse_v[...] * LOG2E

    def grads_out(b, dev):
        for g in range(groups):
            gsend[b - 1, :, pl.ds(g * HEAD, HEAD)] = dk[b, g].astype(BF16)
            gsend[b - 1, :, pl.ds((groups + g) * HEAD, HEAD)] = dv[b, g].astype(BF16)
        return remote(gsend.at[b - 1], grecv.at[b - 1], g_send.at[b - 1], g_recv.at[b - 1], {"seq": dev})

    steps = 3 * heads

    def attn_step(it, _):
        b = it // heads
        h = lax.rem(it, heads)
        g = h // per
        for s in range(steps):
            if attn_at.get(s) or s % heads == 0:
                @pl.when(it == s)
                def _(s=s):
                    for ev in attn_at.get(s, ()):
                        event(*ev)
                    if s % heads == 0:
                        bb = s // heads
                        if bb:
                            halo[2 * (bb - 1)].wait_recv()
                            halo[2 * (bb - 1) + 1].wait_recv()
                        for gg in range(groups):
                            kt[gg] = kb[bb, :, pl.ds(gg * HEAD, HEAD)].astype(F32).T.astype(BF16)
                        if bb == 2:
                            grads_out(1, prv1).start()
        cols = pl.ds(pl.multiple_of(h * HEAD, HEAD), HEAD)
        gcols = pl.ds(pl.multiple_of(g * HEAD, HEAD), HEAD)
        qh = qv[:, cols]
        doh = dov[:, cols]
        sc = lax.dot_general(kb[b, :, gcols], qh, NT, preferred_element_type=F32)
        p = jnp.exp2((sc * (scale * LOG2E) - lse_v[pl.ds(h, 1), :]) + bias[b])
        dv[b, g] += jnp.dot(p.astype(BF16), doh, preferred_element_type=F32)
        dp = lax.dot_general(vb[b, :, gcols], doh, NT, preferred_element_type=F32)
        ds = (p * (dp - stat[h, pl.ds(0, 1), :]) * scale).astype(BF16)
        dk[b, g] += jnp.dot(ds, qh, preferred_element_type=F32)
        dq[h] += jnp.dot(kt[g], ds, preferred_element_type=F32)
        return 0

    lax.fori_loop(0, steps, attn_step, 0)
    grads_out(2, prv2).start()

    def to_gt(h, _):
        gt[pl.ds(pl.multiple_of(h * HEAD, HEAD), HEAD), :] = dq[h].astype(BF16)
        return 0

    lax.fori_loop(0, heads, to_gt, 0)

    early, by_group = post
    for ev in early:
        event(*ev)
    for b in (1, 2):
        remote(gsend.at[b - 1], grecv.at[b - 1], g_send.at[b - 1], g_recv.at[b - 1], {"seq": sib}).wait_recv()
    for j, acc in enumerate((dk, dv)):
        for g in range(groups):
            c0 = pl.ds((j * groups + g) * HEAD, HEAD)
            tot = acc[0, g] + grecv[0, :, c0].astype(F32) + grecv[1, :, c0].astype(F32)
            gt[pl.ds((heads + j * groups + g) * HEAD, HEAD), :] = tot.T.astype(BF16)

    def group_mz(j):
        return lax.rem(jnp.where(lax.rem(j, 2) == 1, (j + 1) // 2, NZ - j // 2), NZ)

    def sib_wait(part, my, mz):
        buf = wb if part == 1 else wa
        ref = buf.at[core, slot_me]
        remote(ref, ref, sib_send.at[part], sib_recv.at[part, my, mz], {"seq": sib}).wait_recv()

    def project(j, _):
        for jj in range(NZ):
            @pl.when(j == jj)
            def _(jj=jj):
                mzs = (jj + 1) // 2 if jj % 2 else (NZ - jj // 2) % NZ
                for ev in by_group[jj]:
                    event(*ev)
                for part in range(2):
                    for my in range(NY):
                        if (my, mzs) != (0, 0):
                            sib_wait(part, (NY - my) % NY, (NZ - mzs) % NZ)
        mz = group_mz(j)
        parts = []
        for my in range(NY):
            s = slot_of(my, mz)
            parts.append(jnp.concatenate([wa[0, s], wb[0, s], wa[1, s], wb[1, s]], axis=1))
        lhs = jnp.concatenate(parts, axis=0)
        res[...] = jnp.dot(lhs, gt[...], preferred_element_type=F32)
        for my in range(NY):
            s = slot_of(my, mz)
            own = pl.multiple_of(my * 2 * half + half * hd, 8)
            oth = pl.multiple_of(my * 2 * half + half * (1 - hd), 8)
            oacc[pl.ds(pl.multiple_of(s * half, 8), half), :] = res[pl.ds(own, half), :]
            psend[j, my] = res[pl.ds(oth, half), :].astype(BF16)
        remote(psend.at[j], precv.at[j], p_send.at[j], p_recv.at[j], {"head": 1 - hd}).start()
        return 0

    lax.fori_loop(0, NZ, project, 0)

    def finish(j, _):
        remote(psend.at[j], precv.at[j], p_send.at[j], p_recv.at[j], {"head": 1 - hd}).wait_recv()
        mz = group_mz(j)
        for my in range(NY):
            r = pl.ds(pl.multiple_of(slot_of(my, mz) * half, 8), half)
            oacc[r, :] = oacc[r, :] + precv[j, my].astype(F32)
        return 0

    lax.fori_loop(0, NZ, finish, 0)

    def flip(k, _):
        c = pl.ds(pl.multiple_of(k * HEAD, HEAD), HEAD)
        out_ref[:, c] = oacc[c, :].T.astype(BF16)
        return 0

    lax.fori_loop(0, oacc.shape[0] // HEAD, flip, 0)

    for c in stage + halo:
        c.wait_send()
    for part, buf in ((0, wa), (1, wb)):
        many = buf.at[0, pl.ds(0, NY * NZ - 1)]
        for sem in (ici_send, sib_send):
            remote(many, many, sem.at[part], ici_recv.at[part, 0, 0], {"seq": sib}).wait_send()
    for b in (1, 2):
        remote(gsend.at[b - 1], grecv.at[b - 1], g_send.at[b - 1], g_recv.at[b - 1], {"seq": sib}).wait_send()
    for j in range(NZ):
        remote(psend.at[j], precv.at[j], p_send.at[j], p_recv.at[j], {"head": 1 - hd}).wait_send()


def make_plan(size0, size1, steps, attn_start, attn_us, gt_ready):
    order = event_plan(size0, size1)
    attn_at = {-1: []}
    early = []
    late = [[] for _ in range(NZ)]
    rank = {0: 0, 1: 1, 7: 2, 2: 3, 6: 4, 3: 5, 5: 6, 4: 7}
    left = []
    for t, part, my, mz in order:
        s = math.ceil((t - attn_start) / attn_us)
        if s <= 0:
            attn_at.setdefault(-1 if (my, mz) == (0, 0) else 0, []).append((part, my, mz))
        elif s < steps:
            attn_at.setdefault(s, []).append((part, my, mz))
        elif t < gt_ready:
            early.append((part, my, mz))
        else:
            left.append((part, my, mz))
    pos = 0
    for j in range(NZ):
        need = -1
        for i, (part, my, mz) in enumerate(left):
            if rank[mz] <= j or rank[(NZ - mz) % NZ] <= j:
                need = i
        while pos <= need:
            late[j].append(left[pos])
            pos += 1
    assert pos == len(left)
    return attn_at, (early, late)


def shards(query, key, value, output, output_gradient, lse, doc_lengths, w_query, key_weight, value_weight):
    tok = query.shape[0]
    heads = query.shape[1] // HEAD
    groups = key.shape[1] // HEAD
    rows = w_query.shape[0]
    kdim = w_query.shape[1] + key_weight.shape[1] + value_weight.shape[1]
    la = kdim // 6
    lb = kdim // 3
    slots = NY * NZ
    plan = make_plan(4 * rows * la * 2, 4 * rows * lb * 2, 3 * heads, 3.0, 0.4, 30.0)
    any_ = pl.BlockSpec(memory_space=pl.ANY)
    vmem = pl.BlockSpec(memory_space=pltpu.VMEM)
    dma = pltpu.SemaphoreType.DMA
    return pl.pallas_call(
        functools.partial(kernel, plan),
        out_shape=jax.ShapeDtypeStruct((tok, query.shape[1]), BF16),
        in_specs=[any_] * 6 + [pl.BlockSpec(memory_space=pltpu.SMEM)] + [any_] * 3,
        out_specs=vmem,
        scratch_shapes=[
            pltpu.VMEM((tok, heads * HEAD), BF16),
            pltpu.VMEM((tok, heads * HEAD), BF16),
            pltpu.VMEM((tok, heads * HEAD), BF16),
            pltpu.VMEM((3, tok, groups * HEAD), BF16),
            pltpu.VMEM((3, tok, groups * HEAD), BF16),
            pltpu.VMEM((groups, HEAD, tok), BF16),
            pltpu.VMEM((3, tok, tok), F32),
            pltpu.VMEM((heads, 8, tok), F32),
            pltpu.VMEM((heads, tok), F32),
            pltpu.VMEM((heads, HEAD, tok), F32),
            pltpu.VMEM((kdim, tok), BF16),
            pltpu.VMEM((3, groups, tok, HEAD), F32),
            pltpu.VMEM((3, groups, tok, HEAD), F32),
            pltpu.VMEM((2, tok, 2 * groups * HEAD), BF16),
            pltpu.VMEM((2, tok, 2 * groups * HEAD), BF16),
            pltpu.VMEM((4, rows, kdim), BF16),
            pltpu.VMEM((4 * rows, kdim), F32),
            pltpu.VMEM((2, slots, 4 * rows, la), BF16),
            pltpu.VMEM((2, slots, 4 * rows, lb), BF16),
            pltpu.VMEM((NY * 4 * rows, tok), F32),
            pltpu.VMEM((NZ, NY, 2 * rows, tok), BF16),
            pltpu.VMEM((NZ, NY, 2 * rows, tok), BF16),
            pltpu.VMEM((slots * 2 * rows, tok), F32),
            dma((9,)), dma((2, 2)), dma((2, 2)), dma((9,)), dma((9,)),
            dma((2, NY, NZ)), dma((2, NY, NZ)),
            dma((2,)), dma((2,)), dma((2,)), dma((2,)), dma((NZ,)), dma((NZ,)),
        ],
        compiler_params=pltpu.CompilerParams(
            collective_id=0, has_side_effects=True, vmem_limit_bytes=60 * 1024 * 1024
        ),
    )(query, key, value, output, output_gradient, lse, doc_lengths, w_query, key_weight, value_weight)


def solution(mesh):
    both = P("seq", "head")
    in_specs = (both,) * 5 + (P("head", "seq"), P()) + (both,) * 3
    return jax.shard_map(shards, mesh=mesh, in_specs=in_specs, out_specs=both, check_vma=False)
```

```python
import functools
import math

import jax
import jax.numpy as jnp
from jax import lax
from jax.experimental import pallas as pl
from jax.experimental.pallas import tpu as pltpu
from jax.sharding import PartitionSpec as P

HEAD = 128
WINDOW = 512
NEG = -1e30
LOG2E = math.log2(math.e)
F32 = jnp.float32
BF16 = jnp.bfloat16

NY, NZ = 4, 8
LINK = 90e3
HOP = 2.0
LOOK = 4.0
NT = (((1,), (1,)), ((), ()))


def chunk_sends(part, my, mz):
    out = []
    z_up = ("z", 1, my, (mz + 1) % NZ)
    z_dn = ("z", -1, my, (mz - 1) % NZ)
    y_up = ("y", 1, (my + 1) % NY, mz)
    y_dn = ("y", -1, (my - 1) % NY, mz)
    z_ups = mz <= 3
    z_dns = mz == 0 or mz in (6, 7)
    y_ups = my <= 1
    y_dns = my == 0
    if part == 1:
        if my == 0:
            out += [z_up] if z_ups else []
            out += [z_dn] if z_dns else []
        out += [y_up] if y_ups else []
        out += [y_dn] if y_dns else []
    else:
        if mz == 0:
            out += [y_up] if y_ups else []
            out += [y_dn] if y_dns else []
        out += [z_up] if z_ups else []
        out += [z_dn] if z_dns else []
    return out


def priority(part, my, mz):
    near_z = min(mz, NZ - mz)
    near_y = min(my, NY - my)
    return near_z, near_y, part


def event_plan(size0, size1):
    size = (size0, size1)
    free = {"z": 0.0, "y": 0.0}
    queue = {"z": [], "y": []}
    ops = []

    def arrive(t, part, my, mz):
        ops.append((t, 0, "recv", part, my, mz))
        for axis, way, ry, rz in chunk_sends(part, my, mz):
            first = (part == 1) == (axis == "z")
            queue[axis].append((t, (0 if first else 1,) + priority(part, ry, rz), (part, my, mz, axis, way, ry, rz)))

    pending = []
    arrive(0.0, 1, 0, 0)
    arrive(0.0, 0, 0, 0)
    while pending or queue["z"] or queue["y"]:
        best = None
        for axis in ("z", "y"):
            if queue[axis]:
                start = max(free[axis], min(r for r, _, _ in queue[axis]))
                if best is None or start < best[0]:
                    best = (start, axis)
        if pending and (best is None or min(pending)[0] <= best[0]):
            item = min(pending)
            pending.remove(item)
            arrive(*item)
            continue
        start, axis = best
        item = min((q for q in queue[axis] if q[0] <= start), key=lambda q: q[1])
        queue[axis].remove(item)
        ready, _, send = item
        done = start + size[send[0]] / LINK
        free[axis] = done
        pending.append((done + HOP, send[0], send[5], send[6]))
        ops.append((max(ready, start - LOOK), 1, "send") + send)
    ops.sort()
    return ops


def kernel(
    plan,
    q_hbm, k_hbm, v_hbm, o_hbm, do_hbm, lse_hbm, dl_ref, wq_hbm, wk_hbm, wv_hbm,
    out_ref,
    qv, ov, dov, kb, vb, kt, bias, stat, lse_v, dq, gt, dk, dv, nsend, nrecv, gsend, grecv,
    own, st, stf, wa, wb, res, psend, precv, oacc,
    in_sem, kv_send, kv_recv, near_send, near_recv, st_send, st_recv, ici_recv, sib_recv,
    ici_send, sib_send, n_send, n_recv, g_send, g_recv, p_send, p_recv,
):
    tok = qv.shape[0]
    heads = qv.shape[1] // HEAD
    groups = kb.shape[2] // HEAD
    per = heads // groups
    rows, hw = st.shape[1], st.shape[2]
    half = 2 * rows
    scale = 1.0 / math.sqrt(HEAD)
    wq_w, wk_w = wq_hbm.shape[1], wk_hbm.shape[1]

    me = lax.axis_index("seq")
    hd = lax.axis_index("head")
    n = NY * NZ * 4
    core = lax.rem(me, 2)
    zc = lax.rem(me // 2, NZ)
    yc = lax.rem(me // (2 * NZ), NY)
    xc = me // (2 * NZ * NY)
    sg = 1 - 2 * core
    slot_me = yc * NZ + zc
    piece_me = xc * 2 + core

    def at(x, y, z, c):
        return ((x * NY + y) * NZ + z) * 2 + c

    def zn(d):
        return at(xc, yc, lax.rem(zc + d * sg + NZ, NZ), core)

    def yn(d):
        return at(xc, lax.rem(yc + d * sg + NY, NY), zc, core)

    def slot_of(my, mz):
        y = lax.rem(yc - my * sg + NY, NY)
        z = lax.rem(zc - mz * sg + NZ, NZ)
        return y * NZ + z

    sib = at(xc, yc, zc, 1 - core)
    xsame = at(1 - xc, yc, zc, core)
    xother = at(1 - xc, yc, zc, 1 - core)
    nxt, prv = lax.rem(me + 2, n), lax.rem(me + n - 2, n)

    barrier = pltpu.get_barrier_semaphore()
    partners = [sib, xsame, xother, zn(1), zn(-1), yn(1), yn(-1), nxt, prv]
    for d in partners:
        pl.semaphore_signal(barrier, inc=1, device_id={"seq": d}, device_id_type=pl.DeviceIdType.MESH)
    pl.semaphore_signal(barrier, inc=1, device_id={"head": 1 - hd}, device_id_type=pl.DeviceIdType.MESH)

    w_own = [
        pltpu.make_async_copy(wq_hbm.at[:, pl.ds(0, hw)], own.at[0], in_sem.at[6]),
        pltpu.make_async_copy(wq_hbm.at[:, pl.ds(hw, wq_w - hw)], own.at[1, :, pl.ds(0, wq_w - hw)], in_sem.at[7]),
        pltpu.make_async_copy(wk_hbm, own.at[1, :, pl.ds(wq_w - hw, wk_w)], in_sem.at[8]),
        pltpu.make_async_copy(wv_hbm, own.at[1, :, pl.ds(wq_w - hw + wk_w, wk_w)], in_sem.at[9]),
    ]
    kv_own = [
        pltpu.make_async_copy(k_hbm, kb.at[0], in_sem.at[0]),
        pltpu.make_async_copy(v_hbm, vb.at[0], in_sem.at[1]),
    ]
    locals_ = [
        pltpu.make_async_copy(do_hbm, dov, in_sem.at[2]),
        pltpu.make_async_copy(o_hbm, ov, in_sem.at[3]),
        pltpu.make_async_copy(q_hbm, qv, in_sem.at[4]),
        pltpu.make_async_copy(lse_hbm, lse_v, in_sem.at[5]),
    ]
    for c in w_own + kv_own + locals_:
        c.start()

    qpos = me * tok + lax.broadcasted_iota(jnp.int32, (1, tok), 1)
    low = jnp.zeros((1, tok), jnp.int32)
    start = jnp.int32(0)
    for d in range(dl_ref.shape[0]):
        low = jnp.where(qpos >= start, start, low)
        start = start + dl_ref[d]
    low = jnp.maximum(low, qpos - (WINDOW - 1))
    for b in range(3):
        kpos = (me - b) * tok + lax.broadcasted_iota(jnp.int32, (tok, tok), 0)
        ok = (kpos >= low) & (kpos <= qpos)
        bias[b] = jnp.where(ok, 0.0, NEG).astype(F32)
    dk[...] = jnp.zeros_like(dk)
    dv[...] = jnp.zeros_like(dv)
    dq[...] = jnp.zeros_like(dq)

    for c in w_own + kv_own:
        c.wait()
    pl.semaphore_wait(barrier, len(partners) + 1)

    def remote(src, dst, ssem, rsem, dev):
        return pltpu.make_async_remote_copy(
            src_ref=src, dst_ref=dst, send_sem=ssem, recv_sem=rsem,
            device_id=dev, device_id_type=pl.DeviceIdType.MESH,
        )

    stage = [
        remote(own.at[kh], st.at[piece_me], st_send.at[j], st_recv.at[j], {"seq": dev})
        for j, (kh, dev) in enumerate(((core, xsame), (1 - core, xother), (1 - core, sib)))
    ]
    halo = [
        remote(src.at[0], src.at[2], kv_send.at[j], kv_recv.at[j], {"seq": nxt}) for j, src in enumerate((kb, vb))
    ]
    for c in stage + halo:
        c.start()
    mine_in = pltpu.make_async_copy(own.at[core], st.at[piece_me], in_sem.at[10])
    mine_in.start()

    def near_copy(j, src, b):
        return remote(src.at[b], src.at[1], near_send.at[j], near_recv.at[j], {"seq": sib})

    @pl.when(core == 0)
    def _():
        for j, src in enumerate((kb, vb)):
            near_copy(j, src, 0).start()

    for c in stage:
        c.wait_recv()
    mine_in.wait()
    la, lb = wa.shape[3], wb.shape[3]
    for p in range(4):
        stf[pl.ds(p * rows, rows), :] = st[p].astype(F32)
    wb[core, slot_me] = stf[:, pl.ds(la, lb)].astype(BF16)
    wa[core, slot_me] = stf[:, pl.ds(0, la)].astype(BF16)

    def event(kind, part, my, mz, *to):
        buf = wb if part == 1 else wa
        ref = buf.at[core, slot_of(my, mz)]
        if kind == "recv":
            if (my, mz) != (0, 0):
                remote(ref, ref, ici_send.at[part], ici_recv.at[part, my, mz], {"seq": sib}).wait_recv()
            remote(ref, ref, sib_send.at[part], sib_recv.at[part, my, mz], {"seq": sib}).start()
        else:
            axis, way, ry, rz = to
            dev = zn(way) if axis == "z" else yn(way)
            remote(ref, ref, ici_send.at[part], ici_recv.at[part, ry, rz], {"seq": dev}).start()

    attn_at, by_group = plan
    for ev in attn_at[-1]:
        event(*ev)

    for c in locals_:
        c.wait()

    def delta_step(h, _):
        cols = pl.ds(pl.multiple_of(h * HEAD, HEAD), HEAD)
        prod = dov[:, cols].astype(F32) * ov[:, cols].astype(F32)
        hi = prod.astype(BF16)
        lo = (prod - hi.astype(F32)).astype(BF16)
        one = jnp.ones((8, HEAD), BF16)
        tot = lax.dot_general(one, hi, NT, preferred_element_type=F32) + lax.dot_general(one, lo, NT, preferred_element_type=F32)
        stat[h] = tot
        return 0

    lax.fori_loop(0, heads, delta_step, 0)
    lse_v[...] = lse_v[...] * LOG2E

    near_grad = remote(nsend, nrecv, n_send, n_recv, {"seq": sib})
    far_grad = remote(gsend, grecv, g_send, g_recv, {"seq": prv})

    def cols_of(j, g):
        return pl.ds((j * groups + g) * HEAD, HEAD)

    def send_near():
        for j, acc in enumerate((dk, dv)):
            for g in range(groups):
                nsend[:, cols_of(j, g)] = acc[1, g]
        near_grad.start()

    def send_far():
        near_grad.wait_recv()
        keep = (core == 0).astype(F32)
        for j, acc in enumerate((dk, dv)):
            for g in range(groups):
                got = nrecv[:, cols_of(j, g)]
                gsend[:, cols_of(j, g)] = (acc[2, g] + jnp.where(core == 1, got, 0.0)).astype(BF16)
        far_grad.start()

    sub = ((0, 1), (2, 3), (4, 5, 6))
    outer = 3 * groups

    def attn_step(it, _):
        b = 2 - it // groups
        g = lax.rem(it, groups)
        for si, hs in enumerate(sub):
            for o in range(outer):
                todo = attn_at.get(o * len(sub) + si, ())
                first = si == 0
                far_now = o == 2 * groups and si == 2
                if todo or first or far_now:
                    @pl.when(it == o)
                    def _(o=o, todo=todo, first=first, far_now=far_now):
                        for ev in todo:
                            event(*ev)
                        bb = 2 - o // groups
                        if first:
                            if o == 0:
                                for c in halo:
                                    c.wait_recv()

                                @pl.when(core == 1)
                                def _():
                                    for j, src in enumerate((kb, vb)):
                                        near_copy(j, src, 2).start()
                            if o == groups:
                                for j, src in enumerate((kb, vb)):
                                    near_copy(j, src, 0).wait_recv()
                            if o == 2 * groups:
                                send_near()
                            if o % groups == 0:
                                for gg in range(groups):
                                    kt[gg] = kb[bb, :, pl.ds(gg * HEAD, HEAD)].astype(F32).T.astype(BF16)
                        if far_now:
                            send_far()
            gcols = pl.ds(pl.multiple_of(g * HEAD, HEAD), HEAD)
            kg, vg, ktg = kb[b, :, gcols], vb[b, :, gcols], kt[g]
            bs = bias[b]
            dvs, dks = [], []
            for hh in hs:
                h = g * per + hh
                cols = pl.ds(pl.multiple_of(h * HEAD, HEAD), HEAD)
                qh = qv[:, cols]
                doh = dov[:, cols]
                sc = lax.dot_general(kg, qh, NT, preferred_element_type=F32)
                dp = lax.dot_general(vg, doh, NT, preferred_element_type=F32)
                p = jnp.exp2((sc * (scale * LOG2E) - lse_v[pl.ds(h, 1), :]) + bs)
                ds = (p * (dp - stat[h, pl.ds(0, 1), :]) * scale).astype(BF16)
                dvs.append(jnp.dot(p.astype(BF16), doh, preferred_element_type=F32))
                dks.append(jnp.dot(ds, qh, preferred_element_type=F32))
                dq[h] += jnp.dot(ktg, ds, preferred_element_type=F32)
            dv[b, g] += sum(dvs[1:], dvs[0])
            dk[b, g] += sum(dks[1:], dks[0])
        return 0

    lax.fori_loop(0, outer, attn_step, 0)

    def to_gt(h, _):
        gt[pl.ds(pl.multiple_of(h * HEAD, HEAD), HEAD), :] = dq[h].astype(BF16)
        return 0

    lax.fori_loop(0, heads, to_gt, 0)

    far_grad.wait_recv()
    for j, acc in enumerate((dk, dv)):
        for g in range(groups):
            c0 = cols_of(j, g)
            tot = acc[0, g] + grecv[:, c0].astype(F32) + jnp.where(core == 0, nrecv[:, c0], 0.0)
            gt[pl.ds((heads + j * groups + g) * HEAD, HEAD), :] = tot.T.astype(BF16)

    def group_mz(j):
        return lax.rem(jnp.where(lax.rem(j, 2) == 1, (j + 1) // 2, NZ - j // 2), NZ)

    def sib_wait(part, my, mz):
        buf = wb if part == 1 else wa
        ref = buf.at[core, slot_me]
        remote(ref, ref, sib_send.at[part], sib_recv.at[part, my, mz], {"seq": sib}).wait_recv()

    def project(j, _):
        for jj in range(NZ):
            @pl.when(j == jj)
            def _(jj=jj):
                mzs = (jj + 1) // 2 if jj % 2 else (NZ - jj // 2) % NZ
                for ev in by_group[jj]:
                    event(*ev)
                for part in range(2):
                    for my in range(NY):
                        sib_wait(part, (NY - my) % NY, (NZ - mzs) % NZ)
        mz = group_mz(j)
        parts = []
        for my in range(NY):
            s = slot_of(my, mz)
            parts.append(jnp.concatenate([wa[0, s], wb[0, s], wa[1, s], wb[1, s]], axis=1))
        lhs = jnp.concatenate(parts, axis=0)
        res[...] = jnp.dot(lhs, gt[...], preferred_element_type=F32)
        out = []
        for my in range(NY):
            s = slot_of(my, mz)
            mine = pl.multiple_of(my * 2 * half + half * hd, 8)
            oth = pl.multiple_of(my * 2 * half + half * (1 - hd), 8)
            oacc[pl.ds(pl.multiple_of(s * half, 8), half), :] = res[pl.ds(mine, half), :]
            out.append(res[pl.ds(oth, half), :])
        psend[j] = jnp.concatenate(out, axis=0).astype(BF16)
        remote(psend.at[j], precv.at[j], p_send.at[j], p_recv.at[j], {"head": 1 - hd}).start()
        return 0

    lax.fori_loop(0, NZ, project, 0)

    def finish(j, _):
        remote(psend.at[j], precv.at[j], p_send.at[j], p_recv.at[j], {"head": 1 - hd}).wait_recv()
        mz = group_mz(j)
        got = precv[j].astype(F32)
        for my in range(NY):
            r = pl.ds(pl.multiple_of(slot_of(my, mz) * half, 8), half)
            oacc[r, :] = oacc[r, :] + got[my * half : (my + 1) * half]
        return 0

    lax.fori_loop(0, NZ, finish, 0)

    def flip(k, _):
        c = pl.ds(pl.multiple_of(k * HEAD, HEAD), HEAD)
        out_ref[:, c] = oacc[c, :].T.astype(BF16)
        return 0

    lax.fori_loop(0, oacc.shape[0] // HEAD, flip, 0)

    for c in stage + halo + [near_copy(0, kb, 0), near_copy(1, vb, 0), near_grad, far_grad]:
        c.wait_send()
    for part, buf in ((0, wa), (1, wb)):
        for sem, count in ((ici_send, NY * NZ - 1), (sib_send, NY * NZ)):
            many = buf.at[0, pl.ds(0, count)]
            remote(many, many, sem.at[part], ici_recv.at[part, 0, 0], {"seq": sib}).wait_send()
    for j in range(NZ):
        remote(psend.at[j], precv.at[j], p_send.at[j], p_recv.at[j], {"head": 1 - hd}).wait_send()


def make_plan(size0, size1, steps, attn_start, attn_us):
    order = [op[2:] for op in event_plan(size0, size1)]
    times = [op[0] for op in event_plan(size0, size1)]
    attn_at = {}
    left = []
    for t, op in zip(times, order):
        s = math.ceil((t - attn_start) / attn_us)
        if t <= 0.0:
            attn_at.setdefault(-1, []).append(op)
        elif s < steps:
            attn_at.setdefault(max(s, 0), []).append(op)
        else:
            left.append((t, op))
    early, late = [], [[] for _ in range(NZ)]
    rank = {0: 0, 1: 1, 7: 2, 2: 3, 6: 4, 3: 5, 5: 6, 4: 7}
    pos = 0
    for j in range(NZ):
        need = -1
        for i, (_, op) in enumerate(left):
            if op[0] == "recv" and (rank[op[3]] <= j or rank[(NZ - op[3]) % NZ] <= j):
                need = i
        if j == NZ - 1:
            need = len(left) - 1
        while pos <= need:
            late[j].append(left[pos][1])
            pos += 1
    return attn_at, late


def shards(query, key, value, output, output_gradient, lse, doc_lengths, w_query, key_weight, value_weight):
    tok = query.shape[0]
    heads = query.shape[1] // HEAD
    groups = key.shape[1] // HEAD
    rows = w_query.shape[0]
    kdim = w_query.shape[1] + key_weight.shape[1] + value_weight.shape[1]
    la = kdim // 6
    lb = kdim // 3
    slots = NY * NZ
    plan = make_plan(4 * rows * la * 2, 4 * rows * lb * 2, 9 * groups, 4.0, 0.9)
    any_ = pl.BlockSpec(memory_space=pl.ANY)
    vmem = pl.BlockSpec(memory_space=pltpu.VMEM)
    dma = pltpu.SemaphoreType.DMA
    return pl.pallas_call(
        functools.partial(kernel, plan),
        out_shape=jax.ShapeDtypeStruct((tok, query.shape[1]), BF16),
        in_specs=[any_] * 6 + [pl.BlockSpec(memory_space=pltpu.SMEM)] + [any_] * 3,
        out_specs=vmem,
        scratch_shapes=[
            pltpu.VMEM((tok, heads * HEAD), BF16),
            pltpu.VMEM((tok, heads * HEAD), BF16),
            pltpu.VMEM((tok, heads * HEAD), BF16),
            pltpu.VMEM((3, tok, groups * HEAD), BF16),
            pltpu.VMEM((3, tok, groups * HEAD), BF16),
            pltpu.VMEM((groups, HEAD, tok), BF16),
            pltpu.VMEM((3, tok, tok), F32),
            pltpu.VMEM((heads, 8, tok), F32),
            pltpu.VMEM((heads, tok), F32),
            pltpu.VMEM((heads, HEAD, tok), F32),
            pltpu.VMEM((kdim, tok), BF16),
            pltpu.VMEM((3, groups, tok, HEAD), F32),
            pltpu.VMEM((3, groups, tok, HEAD), F32),
            pltpu.VMEM((tok, 2 * groups * HEAD), F32),
            pltpu.VMEM((tok, 2 * groups * HEAD), F32),
            pltpu.VMEM((tok, 2 * groups * HEAD), BF16),
            pltpu.VMEM((tok, 2 * groups * HEAD), BF16),
            pltpu.VMEM((2, rows, kdim // 2), BF16),
            pltpu.VMEM((4, rows, kdim // 2), BF16),
            pltpu.VMEM((4 * rows, kdim // 2), F32),
            pltpu.VMEM((2, slots, 4 * rows, la), BF16),
            pltpu.VMEM((2, slots, 4 * rows, lb), BF16),
            pltpu.VMEM((NY * 4 * rows, tok), F32),
            pltpu.VMEM((NZ, NY * 2 * rows, tok), BF16),
            pltpu.VMEM((NZ, NY * 2 * rows, tok), BF16),
            pltpu.VMEM((slots * 2 * rows, tok), F32),
            dma((11,)), dma((2,)), dma((2,)), dma((2,)), dma((2,)), dma((3,)), dma((3,)),
            dma((2, NY, NZ)), dma((2, NY, NZ)),
            dma((2,)), dma((2,)), dma(()), dma(()), dma(()), dma(()), dma((NZ,)), dma((NZ,)),
        ],
        compiler_params=pltpu.CompilerParams(
            collective_id=0, has_side_effects=True, vmem_limit_bytes=60 * 1024 * 1024
        ),
    )(query, key, value, output, output_gradient, lse, doc_lengths, w_query, key_weight, value_weight)


def solution(mesh):
    both = P("seq", "head")
    in_specs = (both,) * 5 + (P("head", "seq"), P()) + (both,) * 3
    return jax.shard_map(shards, mesh=mesh, in_specs=in_specs, out_specs=both, check_vma=False)
```

```python
import functools
import math

import jax
import jax.numpy as jnp
from jax import lax
from jax.experimental import pallas as pl
from jax.experimental.pallas import tpu as pltpu
from jax.sharding import PartitionSpec as P

HEAD = 128
WINDOW = 512
NEG = -1e30
LOG2E = math.log2(math.e)
F32 = jnp.float32
BF16 = jnp.bfloat16

NY, NZ = 4, 8
LINK = 92e3
HOP = 2.2
LOOK = 10.0
SIB_AFTER = 0.3
NT = (((1,), (1,)), ((), ()))


def chunk_sends(part, my, mz):
    out = []
    z_up = ("z", 1, my, (mz + 1) % NZ)
    z_dn = ("z", -1, my, (mz - 1) % NZ)
    y_up = ("y", 1, (my + 1) % NY, mz)
    y_dn = ("y", -1, (my - 1) % NY, mz)
    z_ups = mz <= 3
    z_dns = mz == 0 or mz in (6, 7)
    y_ups = my <= 1
    y_dns = my == 0
    if part == 1:
        if my == 0:
            out += [z_up] if z_ups else []
            out += [z_dn] if z_dns else []
        out += [y_up] if y_ups else []
        out += [y_dn] if y_dns else []
    else:
        if mz == 0:
            out += [y_up] if y_ups else []
            out += [y_dn] if y_dns else []
        out += [z_up] if z_ups else []
        out += [z_dn] if z_dns else []
    return out


def priority(part, my, mz):
    near_z = min(mz, NZ - mz)
    near_y = min(my, NY - my)
    return near_z, near_y, part


def event_plan(size0, size1, extra):
    size = (size0, size1)
    links = [(axis, way) for axis in ("z", "y") for way in (1, -1)]
    free = dict.fromkeys(links, 0.0)
    free["z", 1] = 2.5
    queue = {link: [] for link in links}
    queue["z", -1] += [(extra[0], (-1,), None, c, extra[1]) for c in range(2)]
    recv, ready_at, begin = {}, {}, {}
    pending = [(own_at, c, part, 0, 0) for c in range(2) for part, own_at in ((0, 0.0), (1, 2.0))]
    while pending or any(queue.values()):
        best = None
        for link in links:
            if queue[link]:
                start = max(free[link], min(q[0] for q in queue[link]))
                if best is None or start < best[0]:
                    best = (start, link)
        if pending and (best is None or min(pending)[0] <= best[0]):
            item = min(pending)
            pending.remove(item)
            t, c, part, my, mz = item
            recv[part, my, mz] = max(t, recv.get((part, my, mz), 0.0))
            for axis, way, ry, rz in chunk_sends(part, my, mz):
                first = (part == 1) == (axis == "z")
                send = (part, my, mz, axis, way, ry, rz)
                link = (axis, way * (1 - 2 * c))
                queue[link].append((t, (0 if first else 1,) + priority(part, ry, rz), send, c, size[part]))
            continue
        start, link = best
        item = min((q for q in queue[link] if q[0] <= start), key=lambda q: q[1])
        queue[link].remove(item)
        _, _, send, c, nbytes = item
        free[link] = start + nbytes / LINK
        if send is not None:
            begin.setdefault(send, []).append(start)
            pending.append((free[link] + HOP, c, send[0], send[5], send[6]))
    ops = [(t, 0, "recv") + key for key, t in recv.items()]
    for send, starts in begin.items():
        ops.append((max(recv[send[:3]], min(starts) - LOOK), 1, "send") + send)
    ops += [(t + SIB_AFTER, 2, "sib") + key for key, t in recv.items()]
    ops.sort()
    return ops


def kernel(
    plan,
    q_hbm, k_hbm, v_hbm, o_hbm, do_hbm, lse_hbm, dl_ref, wq_hbm, wk_hbm, wv_hbm,
    out_ref,
    qv, ov, dov, kb, vb, kt, bias, stat, lse_v, dq, gt, dk, dv, nsend, nrecv, gsend, grecv,
    own, st, stf, wa, wb, res, psend, precv, oacc,
    in_sem, kv_send, kv_recv, near_send, near_recv, st_send, st_recv, ici_recv, sib_recv,
    greet, ici_send, sib_send, n_send, n_recv, g_send, g_recv, p_send, p_recv,
):
    tok = qv.shape[0]
    heads = qv.shape[1] // HEAD
    groups = kb.shape[2] // HEAD
    per = heads // groups
    rows, hw = st.shape[1], st.shape[2]
    half = 2 * rows
    scale = 1.0 / math.sqrt(HEAD)
    wq_w, wk_w = wq_hbm.shape[1], wk_hbm.shape[1]

    me = lax.axis_index("seq")
    hd = lax.axis_index("head")
    n = NY * NZ * 4
    core = lax.rem(me, 2)
    zc = lax.rem(me // 2, NZ)
    yc = lax.rem(me // (2 * NZ), NY)
    xc = me // (2 * NZ * NY)
    sg = 1 - 2 * core
    slot_me = yc * NZ + zc
    piece_me = xc * 2 + core

    def at(x, y, z, c):
        return ((x * NY + y) * NZ + z) * 2 + c

    def zn(d):
        return at(xc, yc, lax.rem(zc + d * sg + NZ, NZ), core)

    def yn(d):
        return at(xc, lax.rem(yc + d * sg + NY, NY), zc, core)

    def slot_of(my, mz):
        y = lax.rem(yc - my * sg + NY, NY)
        z = lax.rem(zc - mz * sg + NZ, NZ)
        return y * NZ + z

    sib = at(xc, yc, zc, 1 - core)
    xsame = at(1 - xc, yc, zc, core)
    xother = at(1 - xc, yc, zc, 1 - core)
    nxt, prv = lax.rem(me + 2, n), lax.rem(me + n - 2, n)

    barrier = pltpu.get_barrier_semaphore()
    def xy(d):
        return at(1 - xc, lax.rem(yc + d + NY, NY), zc, core)

    partners = [sib, xsame, xother, zn(1), zn(-1), yn(1), yn(-1), xy(1), xy(-1)]
    for d in partners:
        pl.semaphore_signal(barrier, inc=1, device_id={"seq": d}, device_id_type=pl.DeviceIdType.MESH)
    pl.semaphore_signal(barrier, inc=1, device_id={"head": 1 - hd}, device_id_type=pl.DeviceIdType.MESH)

    w_own = [
        pltpu.make_async_copy(wq_hbm.at[:, pl.ds(0, hw)], own.at[0], in_sem.at[6]),
        pltpu.make_async_copy(wq_hbm.at[:, pl.ds(hw, wq_w - hw)], own.at[1, :, pl.ds(0, wq_w - hw)], in_sem.at[7]),
        pltpu.make_async_copy(wk_hbm, own.at[1, :, pl.ds(wq_w - hw, wk_w)], in_sem.at[8]),
        pltpu.make_async_copy(wv_hbm, own.at[1, :, pl.ds(wq_w - hw + wk_w, wk_w)], in_sem.at[9]),
    ]
    kv_own = [
        pltpu.make_async_copy(k_hbm, kb.at[0], in_sem.at[0]),
        pltpu.make_async_copy(v_hbm, vb.at[0], in_sem.at[1]),
    ]
    locals_ = [
        pltpu.make_async_copy(do_hbm, dov, in_sem.at[2]),
        pltpu.make_async_copy(o_hbm, ov, in_sem.at[3]),
        pltpu.make_async_copy(q_hbm, qv, in_sem.at[4]),
        pltpu.make_async_copy(lse_hbm, lse_v, in_sem.at[5]),
    ]
    for c in w_own + kv_own + locals_:
        c.start()

    qpos = me * tok + lax.broadcasted_iota(jnp.int32, (1, tok), 1)
    low = jnp.zeros((1, tok), jnp.int32)
    start = jnp.int32(0)
    for d in range(dl_ref.shape[0]):
        low = jnp.where(qpos >= start, start, low)
        start = start + dl_ref[d]
    low = jnp.maximum(low, qpos - (WINDOW - 1))
    for b in range(3):
        kpos = (me - b) * tok + lax.broadcasted_iota(jnp.int32, (tok, tok), 0)
        ok = (kpos >= low) & (kpos <= qpos)
        bias[b] = jnp.where(ok, 0.0, NEG).astype(F32)
    dk[...] = jnp.zeros_like(dk)
    dv[...] = jnp.zeros_like(dv)
    dq[...] = jnp.zeros_like(dq)

    for c in w_own + kv_own:
        c.wait()
    pl.semaphore_wait(barrier, len(partners) + 1)

    def remote(src, dst, ssem, rsem, dev):
        return pltpu.make_async_remote_copy(
            src_ref=src, dst_ref=dst, send_sem=ssem, recv_sem=rsem,
            device_id=dev, device_id_type=pl.DeviceIdType.MESH,
        )

    la, lb = wa.shape[3], wb.shape[3]
    for d in (1, -1):
        pl.semaphore_signal(greet, inc=1, device_id={"seq": zn(d)}, device_id_type=pl.DeviceIdType.MESH)
    stage = []
    for part, cols in enumerate((pl.ds(0, la), pl.ds(la, lb))):
        for j, (kh, dev) in enumerate(((core, xsame), (1 - core, xother), (1 - core, sib))):
            stage.append(
                remote(own.at[kh, :, cols], st.at[piece_me, :, cols], st_send.at[part, j], st_recv.at[part, j], {"seq": dev})
            )
    halo = [
        remote(src.at[0], src.at[2], kv_send.at[j], kv_recv.at[j], {"seq": nxt}) for j, src in enumerate((kb, vb))
    ]
    for c in stage:
        c.start()
    mine_in = pltpu.make_async_copy(own.at[core], st.at[piece_me], in_sem.at[10])
    mine_in.start()
    pl.semaphore_wait(greet, 2)
    for c in halo:
        c.start()

    def near_copy(j, src, b):
        return remote(src.at[b], src.at[1], near_send.at[j], near_recv.at[j], {"seq": sib})

    @pl.when(core == 0)
    def _():
        for j, src in enumerate((kb, vb)):
            near_copy(j, src, 0).start()

    def event(kind, part, my, mz, *to):
        buf = wb if part == 1 else wa
        ref = buf.at[core, slot_of(my, mz)]
        if kind == "recv":
            if (my, mz) != (0, 0):
                remote(ref, ref, ici_send.at[part], ici_recv.at[part, my, mz], {"seq": sib}).wait_recv()
        elif kind == "sib":
            remote(ref, ref, sib_send.at[part], sib_recv.at[part, my, mz], {"seq": sib}).start()
        else:
            axis, way, ry, rz = to
            dev = zn(way) if axis == "z" else yn(way)
            remote(ref, ref, ici_send.at[part], ici_recv.at[part, ry, rz], {"seq": dev}).start()

    attn_at, mid, by_group = plan
    mine_in.wait()
    for part, (buf, cols) in enumerate(((wa, pl.ds(0, la)), (wb, pl.ds(la, lb)))):
        for c in stage[3 * part : 3 * part + 3]:
            c.wait_recv()
        for p in range(4):
            stf[pl.ds(p * rows, rows), cols] = st[p, :, cols].astype(F32)
        buf[core, slot_me] = stf[:, cols].astype(BF16)
        for ev in attn_at[-1]:
            if ev[1] == part:
                event(*ev)

    for c in locals_:
        c.wait()

    def delta_step(h, _):
        cols = pl.ds(pl.multiple_of(h * HEAD, HEAD), HEAD)
        prod = dov[:, cols].astype(F32) * ov[:, cols].astype(F32)
        hi = prod.astype(BF16)
        lo = (prod - hi.astype(F32)).astype(BF16)
        one = jnp.ones((8, HEAD), BF16)
        tot = lax.dot_general(one, hi, NT, preferred_element_type=F32) + lax.dot_general(one, lo, NT, preferred_element_type=F32)
        stat[h] = tot
        return 0

    lax.fori_loop(0, heads, delta_step, 0)
    lse_v[...] = lse_v[...] * LOG2E

    near_grad = remote(nsend, nrecv, n_send, n_recv, {"seq": sib})
    far_grad = remote(gsend, grecv, g_send, g_recv, {"seq": prv})

    def cols_of(j, g):
        return pl.ds((j * groups + g) * HEAD, HEAD)

    def send_near():
        for j, acc in enumerate((dk, dv)):
            for g in range(groups):
                nsend[:, cols_of(j, g)] = acc[1, g]
        near_grad.start()

    def send_far():
        near_grad.wait_recv()
        keep = (core == 0).astype(F32)
        for j, acc in enumerate((dk, dv)):
            for g in range(groups):
                got = nrecv[:, cols_of(j, g)]
                gsend[:, cols_of(j, g)] = (acc[2, g] + jnp.where(core == 1, got, 0.0)).astype(BF16)
        far_grad.start()

    sub = ((0, 1), (2, 3), (4, 5, 6))
    outer = 3 * groups

    def attn_step(it, _):
        b = 2 - it // groups
        g = lax.rem(it, groups)
        for si, hs in enumerate(sub):
            for o in range(outer):
                todo = attn_at.get(o * len(sub) + si, ())
                first = si == 0
                far_now = o == 2 * groups and si == 2
                if todo or first or far_now:
                    @pl.when(it == o)
                    def _(o=o, todo=todo, first=first, far_now=far_now):
                        for ev in todo:
                            event(*ev)
                        bb = 2 - o // groups
                        if first:
                            if o == 0:
                                for c in halo:
                                    c.wait_recv()

                                @pl.when(core == 1)
                                def _():
                                    for j, src in enumerate((kb, vb)):
                                        near_copy(j, src, 2).start()
                            if o == groups:
                                for j, src in enumerate((kb, vb)):
                                    near_copy(j, src, 0).wait_recv()
                            if o == 2 * groups:
                                send_near()
                            if o % groups == 0:
                                for gg in range(groups):
                                    kt[gg] = kb[bb, :, pl.ds(gg * HEAD, HEAD)].astype(F32).T.astype(BF16)
                        if far_now:
                            send_far()
            gcols = pl.ds(pl.multiple_of(g * HEAD, HEAD), HEAD)
            kg, vg, ktg = kb[b, :, gcols], vb[b, :, gcols], kt[g]
            bs = bias[b]
            dvs, dks = [], []
            for hh in hs:
                h = g * per + hh
                cols = pl.ds(pl.multiple_of(h * HEAD, HEAD), HEAD)
                qh = qv[:, cols]
                doh = dov[:, cols]
                sc = lax.dot_general(kg, qh, NT, preferred_element_type=F32)
                dp = lax.dot_general(vg, doh, NT, preferred_element_type=F32)
                p = jnp.exp2((sc * (scale * LOG2E) - lse_v[pl.ds(h, 1), :]) + bs)
                ds = (p * (dp - stat[h, pl.ds(0, 1), :]) * scale).astype(BF16)
                dvs.append(jnp.dot(p.astype(BF16), doh, preferred_element_type=F32))
                dks.append(jnp.dot(ds, qh, preferred_element_type=F32))
                dq[h] += jnp.dot(ktg, ds, preferred_element_type=F32)
            dv[b, g] += sum(dvs[1:], dvs[0])
            dk[b, g] += sum(dks[1:], dks[0])
        return 0

    lax.fori_loop(0, outer, attn_step, 0)

    def to_gt(h, _):
        gt[pl.ds(pl.multiple_of(h * HEAD, HEAD), HEAD), :] = dq[h].astype(BF16)
        return 0

    lax.fori_loop(0, heads, to_gt, 0)

    for ev in mid:
        event(*ev)
    far_grad.wait_recv()
    for j, acc in enumerate((dk, dv)):
        for g in range(groups):
            c0 = cols_of(j, g)
            tot = acc[0, g] + grecv[:, c0].astype(F32) + jnp.where(core == 0, nrecv[:, c0], 0.0)
            gt[pl.ds((heads + j * groups + g) * HEAD, HEAD), :] = tot.T.astype(BF16)

    def group_mz(j):
        return lax.rem(jnp.where(lax.rem(j, 2) == 1, (j + 1) // 2, NZ - j // 2), NZ)

    def sib_wait(part, my, mz):
        buf = wb if part == 1 else wa
        ref = buf.at[core, slot_me]
        remote(ref, ref, sib_send.at[part], sib_recv.at[part, my, mz], {"seq": sib}).wait_recv()

    def project(j, _):
        for jj in range(NZ):
            @pl.when(j == jj)
            def _(jj=jj):
                mzs = (jj + 1) // 2 if jj % 2 else (NZ - jj // 2) % NZ
                for ev in by_group[jj]:
                    event(*ev)
                for part in range(2):
                    for my in range(NY):
                        sib_wait(part, (NY - my) % NY, (NZ - mzs) % NZ)
        mz = group_mz(j)
        parts = []
        for my in range(NY):
            s = slot_of(my, mz)
            parts.append(jnp.concatenate([wa[0, s], wb[0, s], wa[1, s], wb[1, s]], axis=1))
        lhs = jnp.concatenate(parts, axis=0)
        res[...] = jnp.dot(lhs, gt[...], preferred_element_type=F32)
        out = []
        for my in range(NY):
            s = slot_of(my, mz)
            mine = pl.multiple_of(my * 2 * half + half * hd, 8)
            oth = pl.multiple_of(my * 2 * half + half * (1 - hd), 8)
            oacc[pl.ds(pl.multiple_of(s * half, 8), half), :] = res[pl.ds(mine, half), :]
            out.append(res[pl.ds(oth, half), :])
        psend[j] = jnp.concatenate(out, axis=0).astype(BF16)
        remote(psend.at[j], precv.at[j], p_send.at[j], p_recv.at[j], {"head": 1 - hd}).start()
        return 0

    lax.fori_loop(0, NZ, project, 0)

    def finish(j, _):
        remote(psend.at[j], precv.at[j], p_send.at[j], p_recv.at[j], {"head": 1 - hd}).wait_recv()
        mz = group_mz(j)
        got = precv[j].astype(F32)
        for my in range(NY):
            r = pl.ds(pl.multiple_of(slot_of(my, mz) * half, 8), half)
            oacc[r, :] = oacc[r, :] + got[my * half : (my + 1) * half]
        return 0

    lax.fori_loop(0, NZ, finish, 0)

    def flip(k, _):
        c = pl.ds(pl.multiple_of(k * HEAD, HEAD), HEAD)
        out_ref[:, c] = oacc[c, :].T.astype(BF16)
        return 0

    lax.fori_loop(0, oacc.shape[0] // HEAD, flip, 0)

    for c in stage + halo + [near_copy(0, kb, 0), near_copy(1, vb, 0), near_grad, far_grad]:
        c.wait_send()
    for part, buf in ((0, wa), (1, wb)):
        for sem, count in ((ici_send, NY * NZ - 1), (sib_send, NY * NZ)):
            many = buf.at[0, pl.ds(0, count)]
            remote(many, many, sem.at[part], ici_recv.at[part, 0, 0], {"seq": sib}).wait_send()
    for j in range(NZ):
        remote(psend.at[j], precv.at[j], p_send.at[j], p_recv.at[j], {"head": 1 - hd}).wait_send()


def make_plan(size0, size1, halo, steps, attn_start, attn_us, gt_at):
    ops = event_plan(size0, size1, (attn_start + attn_us * (steps - 4), halo))
    attn_at = {-1: []}
    mid, left = [], []
    for t, _, *op in ops:
        s = math.ceil((t - attn_start) / attn_us)
        if s < 0:
            attn_at[-1].append(op)
        elif s < steps:
            attn_at.setdefault(s, []).append(op)
        elif t < gt_at:
            mid.append(op)
        else:
            left.append(op)
    late = [[] for _ in range(NZ)]
    rank = {0: 0, 1: 1, 7: 2, 2: 3, 6: 4, 3: 5, 5: 6, 4: 7}
    pos = 0
    for j in range(NZ):
        need = -1
        for i, op in enumerate(left):
            if op[0] == "sib" and (rank[op[3]] <= j or rank[(NZ - op[3]) % NZ] <= j):
                need = i
        if j == NZ - 1:
            need = len(left) - 1
        while pos <= need:
            late[j].append(left[pos])
            pos += 1
    return attn_at, mid, late


def shards(query, key, value, output, output_gradient, lse, doc_lengths, w_query, key_weight, value_weight):
    tok = query.shape[0]
    heads = query.shape[1] // HEAD
    groups = key.shape[1] // HEAD
    rows = w_query.shape[0]
    kdim = w_query.shape[1] + key_weight.shape[1] + value_weight.shape[1]
    la = kdim // 6
    lb = kdim // 3
    slots = NY * NZ
    halo = 2 * tok * groups * HEAD * 2
    plan = make_plan(4 * rows * la * 2, 4 * rows * lb * 2, halo, 9 * groups, 3.0, 0.6, 20.0)
    any_ = pl.BlockSpec(memory_space=pl.ANY)
    vmem = pl.BlockSpec(memory_space=pltpu.VMEM)
    dma = pltpu.SemaphoreType.DMA
    return pl.pallas_call(
        functools.partial(kernel, plan),
        out_shape=pltpu.VMEM((tok, query.shape[1]), BF16),
        in_specs=[any_] * 6 + [pl.BlockSpec(memory_space=pltpu.SMEM)] + [any_] * 3,
        out_specs=vmem,
        scratch_shapes=[
            pltpu.VMEM((tok, heads * HEAD), BF16),
            pltpu.VMEM((tok, heads * HEAD), BF16),
            pltpu.VMEM((tok, heads * HEAD), BF16),
            pltpu.VMEM((3, tok, groups * HEAD), BF16),
            pltpu.VMEM((3, tok, groups * HEAD), BF16),
            pltpu.VMEM((groups, HEAD, tok), BF16),
            pltpu.VMEM((3, tok, tok), F32),
            pltpu.VMEM((heads, 8, tok), F32),
            pltpu.VMEM((heads, tok), F32),
            pltpu.VMEM((heads, HEAD, tok), F32),
            pltpu.VMEM((kdim, tok), BF16),
            pltpu.VMEM((3, groups, tok, HEAD), F32),
            pltpu.VMEM((3, groups, tok, HEAD), F32),
            pltpu.VMEM((tok, 2 * groups * HEAD), F32),
            pltpu.VMEM((tok, 2 * groups * HEAD), F32),
            pltpu.VMEM((tok, 2 * groups * HEAD), BF16),
            pltpu.VMEM((tok, 2 * groups * HEAD), BF16),
            pltpu.VMEM((2, rows, kdim // 2), BF16),
            pltpu.VMEM((4, rows, kdim // 2), BF16),
            pltpu.VMEM((4 * rows, kdim // 2), F32),
            pltpu.VMEM((2, slots, 4 * rows, la), BF16),
            pltpu.VMEM((2, slots, 4 * rows, lb), BF16),
            pltpu.VMEM((NY * 4 * rows, tok), F32),
            pltpu.VMEM((NZ, NY * 2 * rows, tok), BF16),
            pltpu.VMEM((NZ, NY * 2 * rows, tok), BF16),
            pltpu.VMEM((slots * 2 * rows, tok), F32),
            dma((11,)), dma((2,)), dma((2,)), dma((2,)), dma((2,)), dma((2, 3)), dma((2, 3)),
            dma((2, NY, NZ)), dma((2, NY, NZ)), pltpu.SemaphoreType.REGULAR,
            dma((2,)), dma((2,)), dma(()), dma(()), dma(()), dma(()), dma((NZ,)), dma((NZ,)),
        ],
        compiler_params=pltpu.CompilerParams(
            collective_id=0, has_side_effects=True, vmem_limit_bytes=60 * 1024 * 1024
        ),
    )(query, key, value, output, output_gradient, lse, doc_lengths, w_query, key_weight, value_weight)


def solution(mesh):
    both = P("seq", "head")
    in_specs = (both,) * 5 + (P("head", "seq"), P()) + (both,) * 3
    return jax.shard_map(shards, mesh=mesh, in_specs=in_specs, out_specs=both, check_vma=False)
```

```python
import functools
import math

import jax
import jax.numpy as jnp
from jax import lax
from jax.experimental import pallas as pl
from jax.experimental.pallas import tpu as pltpu
from jax.sharding import PartitionSpec as P

HEAD = 128
WINDOW = 512
NEG = -1e30
LOG2E = math.log2(math.e)
F32 = jnp.float32
BF16 = jnp.bfloat16

NY, NZ = 4, 8
LINK = 92e3
HOP = 2.2
LOOK = 10.0
RANK = {0: 0, 1: 1, 7: 2, 2: 3, 6: 4, 3: 5, 5: 6, 4: 7}
NT = (((1,), (1,)), ((), ()))


def chunk_sends(part, my, mz):
    out = []
    z_up = ("z", 1, my, (mz + 1) % NZ)
    z_dn = ("z", -1, my, (mz - 1) % NZ)
    y_up = ("y", 1, (my + 1) % NY, mz)
    y_dn = ("y", -1, (my - 1) % NY, mz)
    z_ups = mz <= 3
    z_dns = mz == 0 or mz in (5, 6, 7)
    y_ups = my <= 1
    y_dns = my == 0
    if part == 1:
        if my == 0:
            out += [z_up] if z_ups else []
            out += [z_dn] if z_dns else []
        out += [y_up] if y_ups else []
        out += [y_dn] if y_dns else []
    else:
        if mz == 0:
            out += [y_up] if y_ups else []
            out += [y_dn] if y_dns else []
        out += [z_up] if z_ups else []
        out += [z_dn] if z_dns else []
    return out


def priority(part, my, mz):
    return RANK[mz], min(my, NY - my), part


def takes(core, axis, way, rz):
    return axis != "z" or rz != NZ // 2 or (way == 1) == (core == 0)


def event_plan(size0, size1, extra):
    size = (size0, size1)
    links = [(axis, way) for axis in ("z", "y") for way in (1, -1)]
    free = dict.fromkeys(links, 0.0)
    free["z", 1] = 2.5
    queue = {link: [] for link in links}
    queue["z", -1] += [(extra[0], (-1,), None, c, extra[1]) for c in range(2)]
    recv, ready_at, begin = {}, {}, {}
    pending = [(own_at, c, part, 0, 0) for c in range(2) for part, own_at in ((0, 0.0), (1, 2.0))]
    while pending or any(queue.values()):
        best = None
        for link in links:
            if queue[link]:
                start = max(free[link], min(q[0] for q in queue[link]))
                if best is None or start < best[0]:
                    best = (start, link)
        if pending and (best is None or min(pending)[0] <= best[0]):
            item = min(pending)
            pending.remove(item)
            t, c, part, my, mz = item
            recv[part, my, mz] = max(t, recv.get((part, my, mz), 0.0))
            for axis, way, ry, rz in chunk_sends(part, my, mz):
                if not takes(c, axis, way, rz):
                    continue
                first = (part == 1) == (axis == "z")
                send = (part, my, mz, axis, way, ry, rz)
                link = (axis, way * (1 - 2 * c) if axis == "y" else way)
                queue[link].append((t, (0 if first else 1,) + priority(part, ry, rz), send, c, size[part]))
            continue
        start, link = best
        item = min((q for q in queue[link] if q[0] <= start), key=lambda q: q[1])
        queue[link].remove(item)
        _, _, send, c, nbytes = item
        free[link] = start + nbytes / LINK
        if send is not None:
            begin.setdefault(send, []).append(start)
            pending.append((free[link] + HOP, c, send[0], send[5], send[6]))
    ops = [(t, 0, "recv") + key for key, t in recv.items()]
    for send, starts in begin.items():
        ops.append((max(recv[send[:3]], min(starts) - LOOK), 1, "send") + send)
    ops.sort()
    return ops


def kernel(
    plan,
    q_hbm, k_hbm, v_hbm, o_hbm, do_hbm, lse_hbm, dl_ref, wq_hbm, wk_hbm, wv_hbm,
    out_ref,
    qv, ov, dov, kb, vb, kt, bias, stat, lse_v, dq, gt, dk, dv, nsend, nrecv, gsend, grecv,
    own, st, stf, wa, wb, gx, psum, ssend, srecv, psend, precv, oacc,
    in_sem, kv_send, kv_recv, near_send, near_recv, st_send, st_recv, ici_recv,
    greet, ici_send, gx_send, gx_recv, s_send, s_recv, n_send, n_recv, g_send, g_recv, p_send, p_recv,
):
    tok = qv.shape[0]
    heads = qv.shape[1] // HEAD
    groups = kb.shape[2] // HEAD
    per = heads // groups
    rows, hw = st.shape[1], st.shape[2]
    kh_heads = hw // HEAD
    half = 2 * rows
    scale = 1.0 / math.sqrt(HEAD)
    wq_w, wk_w = wq_hbm.shape[1], wk_hbm.shape[1]

    me = lax.axis_index("seq")
    hd = lax.axis_index("head")
    n = NY * NZ * 4
    core = lax.rem(me, 2)
    zc = lax.rem(me // 2, NZ)
    yc = lax.rem(me // (2 * NZ), NY)
    xc = me // (2 * NZ * NY)
    sg = 1 - 2 * core
    piece_me = xc * 2 + core

    def at(x, y, z, c):
        return ((x * NY + y) * NZ + z) * 2 + c

    def zn(d):
        return at(xc, yc, lax.rem(zc + d + NZ, NZ), core)

    def yn(d):
        return at(xc, lax.rem(yc + d * sg + NY, NY), zc, core)

    def slot_of(my, mz):
        y = lax.rem(yc - my * sg + NY, NY)
        z = lax.rem(zc - mz + NZ, NZ)
        return z * NY + y

    sib = at(xc, yc, zc, 1 - core)
    xsame = at(1 - xc, yc, zc, core)
    xother = at(1 - xc, yc, zc, 1 - core)
    nxt, prv = lax.rem(me + 2, n), lax.rem(me + n - 2, n)

    barrier = pltpu.get_barrier_semaphore()
    def xy(d):
        return at(1 - xc, lax.rem(yc + d + NY, NY), zc, core)

    partners = [sib, xsame, xother, zn(1), zn(-1), yn(1), yn(-1), xy(1), xy(-1)]
    for d in partners:
        pl.semaphore_signal(barrier, inc=1, device_id={"seq": d}, device_id_type=pl.DeviceIdType.MESH)
    pl.semaphore_signal(barrier, inc=1, device_id={"head": 1 - hd}, device_id_type=pl.DeviceIdType.MESH)

    w_own = [
        pltpu.make_async_copy(wq_hbm.at[:, pl.ds(0, hw)], own.at[0], in_sem.at[6]),
        pltpu.make_async_copy(wq_hbm.at[:, pl.ds(hw, wq_w - hw)], own.at[1, :, pl.ds(0, wq_w - hw)], in_sem.at[7]),
        pltpu.make_async_copy(wk_hbm, own.at[1, :, pl.ds(wq_w - hw, wk_w)], in_sem.at[8]),
        pltpu.make_async_copy(wv_hbm, own.at[1, :, pl.ds(wq_w - hw + wk_w, wk_w)], in_sem.at[9]),
    ]
    kv_own = [
        pltpu.make_async_copy(k_hbm, kb.at[0], in_sem.at[0]),
        pltpu.make_async_copy(v_hbm, vb.at[0], in_sem.at[1]),
    ]
    locals_ = [
        pltpu.make_async_copy(do_hbm, dov, in_sem.at[2]),
        pltpu.make_async_copy(o_hbm, ov, in_sem.at[3]),
        pltpu.make_async_copy(q_hbm, qv, in_sem.at[4]),
        pltpu.make_async_copy(lse_hbm, lse_v, in_sem.at[5]),
    ]
    for c in w_own + kv_own + locals_:
        c.start()

    qpos = me * tok + lax.broadcasted_iota(jnp.int32, (1, tok), 1)
    low = jnp.zeros((1, tok), jnp.int32)
    start = jnp.int32(0)
    for d in range(dl_ref.shape[0]):
        low = jnp.where(qpos >= start, start, low)
        start = start + dl_ref[d]
    low = jnp.maximum(low, qpos - (WINDOW - 1))
    for b in range(3):
        kpos = (me - b) * tok + lax.broadcasted_iota(jnp.int32, (tok, tok), 0)
        ok = (kpos >= low) & (kpos <= qpos)
        bias[b] = jnp.where(ok, 0.0, NEG).astype(F32)
    dk[...] = jnp.zeros_like(dk)
    dv[...] = jnp.zeros_like(dv)
    dq[...] = jnp.zeros_like(dq)

    for c in w_own + kv_own:
        c.wait()
    pl.semaphore_wait(barrier, len(partners) + 1)

    def remote(src, dst, ssem, rsem, dev):
        return pltpu.make_async_remote_copy(
            src_ref=src, dst_ref=dst, send_sem=ssem, recv_sem=rsem,
            device_id=dev, device_id_type=pl.DeviceIdType.MESH,
        )

    la, lb = wa.shape[2], wb.shape[2]
    for d in (1, -1):
        pl.semaphore_signal(greet, inc=1, device_id={"seq": zn(d)}, device_id_type=pl.DeviceIdType.MESH)
    stage = []
    for part, cols in enumerate((pl.ds(0, la), pl.ds(la, lb))):
        for j, (kh, dev) in enumerate(((core, xsame), (1 - core, xother), (1 - core, sib))):
            stage.append(
                remote(own.at[kh, :, cols], st.at[piece_me, :, cols], st_send.at[part, j], st_recv.at[part, j], {"seq": dev})
            )
    halo = [
        remote(src.at[0], src.at[2], kv_send.at[j], kv_recv.at[j], {"seq": nxt}) for j, src in enumerate((kb, vb))
    ]
    for c in stage:
        c.start()
    mine_in = pltpu.make_async_copy(own.at[core], st.at[piece_me], in_sem.at[10])
    mine_in.start()
    pl.semaphore_wait(greet, 2)
    for c in halo:
        c.start()

    def near_copy(j, src, b):
        return remote(src.at[b], src.at[1], near_send.at[j], near_recv.at[j], {"seq": sib})

    @pl.when(core == 0)
    def _():
        for j, src in enumerate((kb, vb)):
            near_copy(j, src, 0).start()

    def event(kind, part, my, mz, *to):
        buf = wb if part == 1 else wa
        ref = buf.at[slot_of(my, mz)]
        if kind == "recv":
            if (my, mz) != (0, 0):
                remote(ref, ref, ici_send.at[part], ici_recv.at[part, my, mz], {"seq": sib}).wait_recv()
        else:
            axis, way, ry, rz = to
            dev = zn(way) if axis == "z" else yn(way)
            copy = remote(ref, ref, ici_send.at[part], ici_recv.at[part, ry, rz], {"seq": dev})
            if axis == "z" and rz == NZ // 2:
                pl.when(core == (0 if way == 1 else 1))(copy.start)
            else:
                copy.start()

    attn_at, mid, by_group, rest = plan
    mine_in.wait()
    for part, (buf, cols) in enumerate(((wa, pl.ds(0, la)), (wb, pl.ds(la, lb)))):
        for c in stage[3 * part : 3 * part + 3]:
            c.wait_recv()
        for p in range(4):
            stf[pl.ds(p * rows, rows), cols] = st[p, :, cols].astype(F32)
        buf[zc * NY + yc] = stf[:, cols].astype(BF16)
        for ev in attn_at[-1]:
            if ev[1] == part:
                event(*ev)

    for c in locals_:
        c.wait()

    def delta_step(h, _):
        cols = pl.ds(pl.multiple_of(h * HEAD, HEAD), HEAD)
        prod = dov[:, cols].astype(F32) * ov[:, cols].astype(F32)
        hi = prod.astype(BF16)
        lo = (prod - hi.astype(F32)).astype(BF16)
        one = jnp.ones((8, HEAD), BF16)
        tot = lax.dot_general(one, hi, NT, preferred_element_type=F32) + lax.dot_general(one, lo, NT, preferred_element_type=F32)
        stat[h] = tot
        return 0

    lax.fori_loop(0, heads, delta_step, 0)
    lse_v[...] = lse_v[...] * LOG2E

    near_grad = remote(nsend, nrecv, n_send, n_recv, {"seq": sib})
    far_grad = remote(gsend, grecv, g_send, g_recv, {"seq": prv})

    def cols_of(j, g):
        return pl.ds((j * groups + g) * HEAD, HEAD)

    def send_near():
        for j, acc in enumerate((dk, dv)):
            for g in range(groups):
                nsend[:, cols_of(j, g)] = acc[1, g]
        near_grad.start()

    def send_far():
        near_grad.wait_recv()
        keep = (core == 0).astype(F32)
        for j, acc in enumerate((dk, dv)):
            for g in range(groups):
                got = nrecv[:, cols_of(j, g)]
                gsend[:, cols_of(j, g)] = (acc[2, g] + jnp.where(core == 1, got, 0.0)).astype(BF16)
        far_grad.start()

    sub = ((0, 1), (2, 3), (4, 5, 6))
    outer = 3 * groups

    def attn_step(it, _):
        b = 2 - it // groups
        g = lax.rem(it, groups)
        for si, hs in enumerate(sub):
            for o in range(outer):
                todo = attn_at.get(o * len(sub) + si, ())
                first = si == 0
                far_now = o == 2 * groups and si == 2
                if todo or first or far_now:
                    @pl.when(it == o)
                    def _(o=o, todo=todo, first=first, far_now=far_now):
                        for ev in todo:
                            event(*ev)
                        bb = 2 - o // groups
                        if first:
                            if o == 0:
                                for c in halo:
                                    c.wait_recv()

                                @pl.when(core == 1)
                                def _():
                                    for j, src in enumerate((kb, vb)):
                                        near_copy(j, src, 2).start()
                            if o == groups:
                                for j, src in enumerate((kb, vb)):
                                    near_copy(j, src, 0).wait_recv()
                            if o == 2 * groups:
                                send_near()
                            if o % groups == 0:
                                for gg in range(groups):
                                    kt[gg] = kb[bb, :, pl.ds(gg * HEAD, HEAD)].astype(F32).T.astype(BF16)
                        if far_now:
                            send_far()
            gcols = pl.ds(pl.multiple_of(g * HEAD, HEAD), HEAD)
            kg, vg, ktg = kb[b, :, gcols], vb[b, :, gcols], kt[g]
            bs = bias[b]
            dvs, dks = [], []
            for hh in hs:
                h = g * per + hh
                cols = pl.ds(pl.multiple_of(h * HEAD, HEAD), HEAD)
                qh = qv[:, cols]
                doh = dov[:, cols]
                sc = lax.dot_general(kg, qh, NT, preferred_element_type=F32)
                dp = lax.dot_general(vg, doh, NT, preferred_element_type=F32)
                p = jnp.exp2((sc * (scale * LOG2E) - lse_v[pl.ds(h, 1), :]) + bs)
                ds = (p * (dp - stat[h, pl.ds(0, 1), :]) * scale).astype(BF16)
                dvs.append(jnp.dot(p.astype(BF16), doh, preferred_element_type=F32))
                dks.append(jnp.dot(ds, qh, preferred_element_type=F32))
                dq[h] += jnp.dot(ktg, ds, preferred_element_type=F32)
            dv[b, g] += sum(dvs[1:], dvs[0])
            dk[b, g] += sum(dks[1:], dks[0])
        return 0

    lax.fori_loop(0, outer, attn_step, 0)

    def to_gt(h, _):
        gt[h // kh_heads, pl.ds(pl.multiple_of(lax.rem(h, kh_heads) * HEAD, HEAD), HEAD), :] = dq[h].astype(BF16)
        return 0

    lax.fori_loop(0, heads, to_gt, 0)

    for ev in mid:
        event(*ev)
    far_grad.wait_recv()
    for j, acc in enumerate((dk, dv)):
        for g in range(groups):
            c0 = cols_of(j, g)
            tot = acc[0, g] + grecv[:, c0].astype(F32) + jnp.where(core == 0, nrecv[:, c0], 0.0)
            gt[1, pl.ds((heads + j * groups + g - kh_heads) * HEAD, HEAD), :] = tot.T.astype(BF16)
    gx_copy = remote(gt.at[1 - core], gx, gx_send, gx_recv, {"seq": sib})
    gx_copy.start()
    gx_copy.wait_recv()

    def group_mz(j):
        return lax.rem(jnp.where(lax.rem(j, 2) == 1, (j + 1) // 2, NZ - j // 2), NZ)

    def z_of(j):
        return lax.rem(zc - group_mz(j) + NZ, NZ)

    def quad(za):
        return pl.ds(za * NY, NY)

    def sums(where, k):
        return remote(ssend.at[where], srecv.at[where], s_send.at[k], s_recv.at[k], {"seq": sib})

    def across(where, k):
        return remote(psend.at[where], precv.at[where], p_send.at[k], p_recv.at[k], {"head": 1 - hd})

    def orow(y, za):
        return pl.ds(pl.multiple_of((y * NZ + za) * half, 8), half)

    def total(y, za):
        slot = za * NY + y
        tot = psum[slot] + srecv[slot].astype(F32)
        lo, hi = tot[:half], tot[half:]
        oacc[orow(y, za), :] = jnp.where(hd == 0, lo, hi)
        psend[slot] = jnp.where(hd == 0, hi, lo).astype(BF16)

    def add(y, za):
        oacc[orow(y, za), :] = oacc[orow(y, za), :] + precv[za * NY + y].astype(F32)

    def multiply(ys, za):
        slots = [za * NY + y for y in ys]
        lhs = jnp.concatenate([jnp.concatenate([wa[i], wb[i]], axis=1) for i in slots], axis=0)
        n_rows = 4 * rows
        other = jnp.dot(lhs, gx[...], preferred_element_type=F32).astype(BF16)
        for k, i in enumerate(slots):
            ssend[i] = other[k * n_rows : (k + 1) * n_rows]
        return lhs, slots, n_rows

    def keep(lhs, slots, n_rows):
        mine = jnp.dot(lhs, gt[core], preferred_element_type=F32)
        for k, i in enumerate(slots):
            psum[i] = mine[k * n_rows : (k + 1) * n_rows]

    def late_op(kind, j):
        za = z_of(jnp.int32(j))
        if kind == "sum":
            sums(quad(za), za).wait_recv()
            for y in range(NY):
                total(y, za)
            across(quad(za), za).start()
        else:
            across(quad(za), za).wait_recv()
            for y in range(NY):
                add(y, za)

    def run(ops):
        for ev in ops:
            if ev[0] in ("sum", "add"):
                late_op(*ev)
            else:
                event(*ev)

    def project(j, _):
        for jj in range(NZ - 1):
            if by_group[jj]:
                @pl.when(j == jj)
                def _(jj=jj):
                    run(by_group[jj])
        za = z_of(j)
        state = multiply(list(range(NY)), za)
        sums(quad(za), za).start()
        keep(*state)
        return 0

    def flip(k, _):
        c = pl.ds(pl.multiple_of(k * HEAD, HEAD), HEAD)
        out_ref[:, c] = oacc[c, :].T.astype(BF16)
        return 0

    lax.fori_loop(0, NZ - 1, project, 0)

    last = lax.rem(zc + NZ // 2, NZ)
    far_y = lax.rem(yc + NY // 2, NY)
    near_ys = [lax.rem(yc + d, NY) for d in range(NY) if d != NY // 2]
    run(by_group[NZ - 1])
    state = multiply(near_ys, last)
    for y in near_ys:
        sums(last * NY + y, NZ + y).start()
    keep(*state)
    run(by_group[NZ])
    state = multiply([far_y], last)
    sums(last * NY + far_y, NZ + far_y).start()
    keep(*state)
    run([op for op in rest if op[0] == "sum"])
    for y in near_ys + [far_y]:
        sums(last * NY + y, NZ + y).wait_recv()
        total(y, last)
        across(last * NY + y, NZ + y).start()
    run([op for op in rest if op[0] == "add"])
    for y in near_ys:
        across(last * NY + y, NZ + y).wait_recv()
        add(y, last)
    lax.fori_loop(0, oacc.shape[0] // HEAD, flip, 0)
    across(last * NY + far_y, NZ + far_y).wait_recv()
    add(far_y, last)
    first_row = (far_y * NZ + last) * half
    flip(first_row // HEAD, 0)
    flip((first_row + half - 1) // HEAD, 0)

    for c in stage + halo + [near_copy(0, kb, 0), near_copy(1, vb, 0), near_grad, far_grad]:
        c.wait_send()
    gx_copy.wait_send()
    for pt, buf in ((0, wa), (1, wb)):
        many = buf.at[pl.ds(0, NY * NZ - 1)]
        remote(many, many, ici_send.at[pt], ici_recv.at[pt, 0, 0], {"seq": sib}).wait_send()
    for j in range(NZ - 1):
        za = z_of(jnp.int32(j))
        sums(quad(za), za).wait_send()
        across(quad(za), za).wait_send()
    for y in range(NY):
        sums(last * NY + y, NZ + y).wait_send()
        across(last * NY + y, NZ + y).wait_send()


def make_plan(size0, size1, halo, steps, attn_start, attn_us, gt_at):
    ops = event_plan(size0, size1, (attn_start + attn_us * (steps - 4), halo))
    attn_at = {-1: []}
    mid, left = [], []
    for t, _, *op in ops:
        s = math.ceil((t - attn_start) / attn_us)
        if s < 0:
            attn_at[-1].append(op)
        elif s < steps:
            attn_at.setdefault(s, []).append(op)
        elif t < gt_at:
            mid.append(op)
        else:
            left.append((t, op))
    stages = NZ + 1
    need = [-1] * stages
    at = [0.0] * stages
    for j in range(stages):
        for i, (t, op) in enumerate(left):
            rank = stages - 1 if op[2:4] == [NY // 2, NZ // 2] else RANK[op[3]]
            if op[0] == "recv" and rank <= j:
                need[j] = i
        at[j] = max(left[need[j]][0] if need[j] >= 0 else 0.0, gt_at + 1.5 * (j + 1))
    late = [[] for _ in range(stages)]
    extra = []
    for j in range(NZ - 1):
        t = at[j] + 3.0
        extra += [(t, j + 1, ["sum", j]), (t + 6.0, j + 1, ["add", j])]
    extra.sort()
    pos = 0
    for j in range(stages):
        upto = need[j] if j < stages - 1 else len(left) - 1
        while True:
            ev = left[pos] if pos <= upto else None
            ex = extra[0] if extra and extra[0][1] <= j else None
            if ex and ex[0] < (ev[0] if ev else at[j]):
                late[j].append(ex[2])
                extra.pop(0)
            elif ev:
                late[j].append(ev[1])
                pos += 1
            else:
                break
    assert pos == len(left)
    return attn_at, mid, late, [ex[2] for ex in extra]


def shards(query, key, value, output, output_gradient, lse, doc_lengths, w_query, key_weight, value_weight):
    tok = query.shape[0]
    heads = query.shape[1] // HEAD
    groups = key.shape[1] // HEAD
    rows = w_query.shape[0]
    kdim = w_query.shape[1] + key_weight.shape[1] + value_weight.shape[1]
    la = kdim // 6
    lb = kdim // 3
    slots = NY * NZ
    halo = 2 * tok * groups * HEAD * 2
    plan = make_plan(4 * rows * la * 2, 4 * rows * lb * 2, halo, 9 * groups, 3.0, 0.6, 20.0)
    any_ = pl.BlockSpec(memory_space=pl.ANY)
    vmem = pl.BlockSpec(memory_space=pltpu.VMEM)
    dma = pltpu.SemaphoreType.DMA
    return pl.pallas_call(
        functools.partial(kernel, plan),
        out_shape=pltpu.VMEM((tok, query.shape[1]), BF16),
        in_specs=[any_] * 6 + [pl.BlockSpec(memory_space=pltpu.SMEM)] + [any_] * 3,
        out_specs=vmem,
        scratch_shapes=[
            pltpu.VMEM((tok, heads * HEAD), BF16),
            pltpu.VMEM((tok, heads * HEAD), BF16),
            pltpu.VMEM((tok, heads * HEAD), BF16),
            pltpu.VMEM((3, tok, groups * HEAD), BF16),
            pltpu.VMEM((3, tok, groups * HEAD), BF16),
            pltpu.VMEM((groups, HEAD, tok), BF16),
            pltpu.VMEM((3, tok, tok), F32),
            pltpu.VMEM((heads, 8, tok), F32),
            pltpu.VMEM((heads, tok), F32),
            pltpu.VMEM((heads, HEAD, tok), F32),
            pltpu.VMEM((2, kdim // 2, tok), BF16),
            pltpu.VMEM((3, groups, tok, HEAD), F32),
            pltpu.VMEM((3, groups, tok, HEAD), F32),
            pltpu.VMEM((tok, 2 * groups * HEAD), F32),
            pltpu.VMEM((tok, 2 * groups * HEAD), F32),
            pltpu.VMEM((tok, 2 * groups * HEAD), BF16),
            pltpu.VMEM((tok, 2 * groups * HEAD), BF16),
            pltpu.VMEM((2, rows, kdim // 2), BF16),
            pltpu.VMEM((4, rows, kdim // 2), BF16),
            pltpu.VMEM((4 * rows, kdim // 2), F32),
            pltpu.VMEM((slots, 4 * rows, la), BF16),
            pltpu.VMEM((slots, 4 * rows, lb), BF16),
            pltpu.VMEM((kdim // 2, tok), BF16),
            pltpu.VMEM((slots, 4 * rows, tok), F32),
            pltpu.VMEM((slots, 4 * rows, tok), BF16),
            pltpu.VMEM((slots, 4 * rows, tok), BF16),
            pltpu.VMEM((slots, 2 * rows, tok), BF16),
            pltpu.VMEM((slots, 2 * rows, tok), BF16),
            pltpu.VMEM((slots * 2 * rows, tok), F32),
            dma((11,)), dma((2,)), dma((2,)), dma((2,)), dma((2,)), dma((2, 3)), dma((2, 3)),
            dma((2, NY, NZ)), pltpu.SemaphoreType.REGULAR,
            dma((2,)), dma(()), dma(()), dma((NZ + NY,)), dma((NZ + NY,)), dma(()), dma(()), dma(()), dma(()), dma((NZ + NY,)), dma((NZ + NY,)),
        ],
        compiler_params=pltpu.CompilerParams(
            collective_id=0, has_side_effects=True, vmem_limit_bytes=60 * 1024 * 1024
        ),
    )(query, key, value, output, output_gradient, lse, doc_lengths, w_query, key_weight, value_weight)


def solution(mesh):
    both = P("seq", "head")
    in_specs = (both,) * 5 + (P("head", "seq"), P()) + (both,) * 3
    return jax.shard_map(shards, mesh=mesh, in_specs=in_specs, out_specs=both, check_vma=False)
```
